512 devices in a mesh: rep: 8 (over z_hi, core), dp: 64 (over z_lo, x, y).
Axes of the slice: x: 4, y: 8, z: 8 (z_hi: 4, z_lo: 2; z = z_hi * 2 + z_lo), core: 2. Of those that a mesh axis runs over, the one named last changes fastest.
Arguments:
- frames: bfloat16 [98304, 1536], P(('rep', 'dp')), may hold values from -6 to 6
- lengths: int32 [512, 8], P(('rep', 'dp')), may hold values from 0 to 192, as said below
- destination: int32 [512, 48], P(('rep', 'dp')), may hold values from -1 to 63, as said below
- kernel: float32 [15, 1536], replicated, may hold values from -1.5 to 1.5
- norm_gain: float32 [1536], replicated, may hold values from 0.5 to 1.5
- master: float32 [1536, 1536], P('dp'), may hold values from -0.15625 to 0.15625
- moment: float32 [1536, 1536], P('dp'), may hold values from -0.18 to 0.18
- second: float32 [1536, 1536], P('dp'), may hold values from 0.0003 to 0.003
- gradient: float32 [1536, 1536], P('dp'), may hold values from -1.8 to 1.8
- bucket_order: int32 [64], replicated, may hold values from 0 to 63, each once
- cotangent: bfloat16 [65536, 1536], P(('rep', 'dp')), may hold values from -6 to 6
Outputs:
- projected: bfloat16 [65536, 1536], P(('rep', 'dp'))
- frame_grad: bfloat16 [98304, 1536], P(('rep', 'dp'))
- kernel_grad: float32 [15, 1536], replicated
- gain_grad: float32 [1536], replicated
- new_master: float32 [1536, 1536], P('dp')
The draws below stay inside these ranges and needn't reach their ends.
Inputs may be any that keep to these rules, and one draw needn't show every extreme that they name: destination[i, b] is the device of i's replica group that takes block b of device i, or -1 for a block without frames; a device's blocks with frames come first and go to distinct devices; every device receives exactly 32 blocks. A device's lengths add up to 4 times the number of its blocks that destination sends.
All inputs are finite; a program needn't handle non-finite values.
Results may differ from the reference program's by a relative error of at most 0.012.
Values may be sent and summed in bfloat16 or wider, within the bound.
No kernel may reach another device: no remote copies, remote signals or barrier semaphores. Data moves between devices by JAX's collectives and lax.ppermute only.
A program may use at most 128 MiB of HBM per device.

```python
import math
import jax
import jax.numpy as jnp
from jax import lax

D = 1536
KW = 15
UTT = 8
REPLICAS = 8
OWNERS = 64
MEANB = 32
NB = 48
BLK = 4
FRAMES = 65536
N_REP = 8
N_DP = 64


def group_plan(group_key):
    key_perm, key_delta, key_shift, key_cuts = jax.random.split(group_key, 4)
    ordering = jax.random.permutation(key_perm, jnp.arange(OWNERS, dtype=jnp.int32))
    half_count = OWNERS // 2
    extent = NB - MEANB
    delta = jax.random.randint(key_delta, (half_count,), -extent, extent + 1).astype(jnp.int32).at[0].set(extent)
    counts = jnp.zeros((OWNERS,), jnp.int32).at[ordering[0::2]].set(MEANB + delta).at[ordering[1::2]].set(MEANB - delta)
    ordered = counts[ordering]
    starts_ordered = jnp.cumsum(ordered) - ordered
    position = jnp.argsort(ordering).astype(jnp.int32)
    starts = starts_ordered[position]
    offset = jax.random.randint(key_shift, (), 0, OWNERS).astype(jnp.int32)
    block_index = jnp.arange(NB, dtype=jnp.int32)
    dest_table = jnp.where(block_index[None, :] < counts[:, None], (starts[:, None] + block_index[None, :] + offset) % OWNERS, -1).astype(jnp.int32)
    totals = counts * BLK
    cuts = jax.random.randint(key_cuts, (OWNERS, UTT - 1), 0, NB * BLK + 1).astype(jnp.int32)
    cuts = jnp.minimum(cuts, totals[:, None])
    cuts = jnp.where(jnp.arange(OWNERS, dtype=jnp.int32)[:, None] == ordering[0], 0, cuts)
    cuts = jnp.sort(cuts, axis=1)
    edges = jnp.concatenate([jnp.zeros((OWNERS, 1), jnp.int32), cuts, totals[:, None]], axis=1)
    length_table = (edges[:, 1:] - edges[:, :-1]).astype(jnp.int32)
    return (dest_table, length_table)


def plan_tables(key):
    base_key = jax.random.fold_in(key, 7)
    group_keys = jax.random.split(base_key, REPLICAS)
    return jax.vmap(group_plan)(group_keys)


def draw_destination(key, part):
    dest_table, length_table = plan_tables(key)
    return dest_table.reshape(REPLICAS * OWNERS, NB)


def draw_lengths(key, part):
    dest_table, length_table = plan_tables(key)
    return length_table.reshape(REPLICAS * OWNERS, UTT)


def steps_of(rng, shape, pieces, low, top_value):
    gain, own = 1.0, jax.random.fold_in(rng, 6)
    for axis_at, parts in pieces:
        heights = jnp.exp(jax.random.uniform(jax.random.fold_in(own, axis_at), (parts,), jnp.float32, low / len(pieces), top_value / len(pieces)))
        gain = gain * jnp.repeat(heights, shape[axis_at] // parts).reshape([-1 if axis == axis_at else 1 for axis in range(len(shape))])
    return gain


def scatter_about(own_key, shape, deviation, limit, cuts=(), held_as=jnp.bfloat16):
    drawn = jax.random.normal(own_key, shape, jnp.float32) * deviation
    if len(cuts) > 0:
        drawn = steps_of(own_key, shape, cuts, -0.22, 0.18) * drawn
    return jnp.clip(drawn, min=-limit, max=limit).astype(held_as)


def setup_inputs(seed: int = 0) -> dict:
    key_list = jax.random.split(jax.random.key(seed), 12)
    frames = scatter_about(key_list[0], (N_REP * N_DP * NB * BLK, D), 1.0, 6.0, ((0, 512),))
    lengths = draw_lengths(jax.random.fold_in(key_list[11], 71), 0)
    destination = draw_destination(jax.random.fold_in(key_list[11], 71), 0)
    kernel = scatter_about(key_list[3], (KW, D), KW ** -0.5, 1.5, (), jnp.float32)
    norm_gain = jnp.clip(1.0 + 0.1 * jax.random.normal(key_list[4], (D,), jnp.float32), 0.5, 1.5)
    master = scatter_about(key_list[5], (D, D), D ** -0.5, 0.15625, ((0, 64),), jnp.float32)
    moment = scatter_about(key_list[6], (D, D), 0.03, 0.18, ((0, 64),), jnp.float32)
    second = jnp.clip(jnp.exp(math.log(0.003) - 2.3025851 * jax.random.uniform(key_list[7], (D, D), jnp.float32) ** steps_of(key_list[7], (D, D), ((0, 64),), -0.2, 0.2)), 0.0003, 0.003)
    gradient = scatter_about(key_list[8], (D, D), 0.3, 1.8, ((0, 64),), jnp.float32)
    bucket_order = jax.random.permutation(key_list[9], N_DP).astype(jnp.int32)
    cotangent = scatter_about(key_list[10], (N_REP * N_DP * MEANB * BLK, D), 1.0, 6.0, ((0, 512),))
    return dict(frames=frames, lengths=lengths, destination=destination, kernel=kernel, norm_gain=norm_gain, master=master, moment=moment, second=second, gradient=gradient, bucket_order=bucket_order, cotangent=cotangent)


def adam_step(master, moment, second, gradient):
    moment_new = 0.9 * moment + 0.1 * gradient
    second_new = 0.999 * second + 0.001 * jnp.square(gradient)
    return master - 0.01 * (moment_new / (jnp.sqrt(second_new) + 1e-08) + 0.1 * master)

def layout(lengths_row, height):
    bounds = jnp.cumsum(lengths_row).astype(jnp.int32)
    position = jnp.arange(height, dtype=jnp.int32)
    segment = lax.optimization_barrier(jnp.sum((position[:, None] >= bounds[None, :]).astype(jnp.int32), axis=1)).astype(jnp.int32)
    living = (position < bounds[-1]).astype(jnp.float32)
    return (segment, living)

def activate(frames_f, kernel, norm_gain, segment, living):
    height = frames_f.shape[0]
    half_width = (kernel.shape[0] - 1) // 2
    padded = jnp.pad(frames_f, ((half_width, half_width), (0, 0)))
    padded_seg = jnp.pad(segment, (half_width, half_width), constant_values=-1)
    mixed_sum = jnp.zeros_like(frames_f)
    for tap_index in range(kernel.shape[0]):
        inside = (lax.slice_in_dim(padded_seg, tap_index, tap_index + height) == segment).astype(frames_f.dtype)
        mixed_sum = mixed_sum + kernel[tap_index] * lax.slice_in_dim(padded, tap_index, tap_index + height) * inside[:, None]
    mixed_sum = mixed_sum * living[:, None]
    center = lax.optimization_barrier(jnp.mean(mixed_sum, axis=1, keepdims=True))
    spread = lax.optimization_barrier(jnp.mean(jnp.square(mixed_sum - center), axis=1, keepdims=True))
    scaled = (mixed_sum - center) * lax.rsqrt(spread + 1e-05) * norm_gain
    return scaled * jax.nn.sigmoid(scaled)

def reference(frames, lengths, destination, kernel, norm_gain, master, moment, second, gradient, bucket_order, cotangent):
    updated = adam_step(master, moment, second, gradient)
    bucket_rows = D // OWNERS
    weight = updated.astype(jnp.bfloat16).reshape(OWNERS, bucket_rows, D)[bucket_order].reshape(D, D)
    height = NB * BLK
    frames_group = frames.reshape(REPLICAS, OWNERS, height, D)
    lengths_group = lengths.reshape(REPLICAS, OWNERS, UTT)
    dest_group = destination.reshape(REPLICAS, OWNERS, NB)
    cot_group = cotangent.reshape(REPLICAS, OWNERS * MEANB * BLK, D)

    def one_group(operands):
        group_frames, group_lengths, group_dest, group_cot = operands

        def forward_one(inner):
            frames_one, lengths_one = inner
            segment, living = layout(lengths_one, height)
            return activate(frames_one.astype(jnp.float32), kernel, norm_gain, segment, living).astype(jnp.bfloat16)
        moved_rows = lax.map(forward_one, (group_frames, group_lengths))
        targets = jnp.arange(OWNERS, dtype=jnp.int32)
        sending = jnp.any(group_dest[:, :, None] == targets[None, None, :], axis=1).astype(jnp.int32)
        ranking = jnp.cumsum(sending, axis=0) - sending
        clipped = jnp.maximum(group_dest, 0).astype(jnp.int32)
        slot_index = jnp.where(group_dest >= 0, clipped * MEANB + jnp.take_along_axis(ranking, clipped, axis=1), OWNERS * MEANB).astype(jnp.int32)
        received = jnp.zeros((OWNERS * MEANB + 1, BLK, D), jnp.bfloat16).at[slot_index.reshape(-1)].set(moved_rows.reshape(OWNERS * NB, BLK, D))[:-1]
        projected_rows = jnp.dot(received.reshape(-1, D), weight, preferred_element_type=jnp.float32).astype(jnp.bfloat16)
        back_rows = jnp.dot(group_cot, weight.T, preferred_element_type=jnp.float32).astype(jnp.bfloat16)
        back_padded = jnp.concatenate([back_rows.reshape(OWNERS * MEANB, BLK, D), jnp.zeros((1, BLK, D), jnp.bfloat16)], axis=0)
        returned = back_padded[slot_index.reshape(-1)].reshape(OWNERS, height, D)

        def backward_one(inner):
            frames_one, lengths_one, returned_one = inner
            segment, living = layout(lengths_one, height)
            _, pullback = jax.vjp(lambda inputs, kernel_in, gain_in: activate(inputs, kernel_in, gain_in, segment, living), frames_one.astype(jnp.float32), kernel, norm_gain)
            frame_term, kernel_term, gain_term = pullback(returned_one.astype(jnp.float32))
            return (frame_term.astype(jnp.bfloat16), kernel_term, gain_term)
        frame_grads, kernel_parts, gain_parts = lax.map(backward_one, (group_frames, group_lengths, returned))
        return (projected_rows, frame_grads, lax.optimization_barrier(jnp.sum(kernel_parts, axis=0)), lax.optimization_barrier(jnp.sum(gain_parts, axis=0)))
    projected_all, frame_all, kernel_all, gain_all = lax.map(one_group, (frames_group, lengths_group, dest_group, cot_group))
    divisor = jnp.sqrt(jnp.asarray(FRAMES, jnp.float32))
    return (projected_all.reshape(-1, D), frame_all.reshape(-1, D), lax.optimization_barrier(jnp.sum(kernel_all, axis=0)) / divisor, lax.optimization_barrier(jnp.sum(gain_all, axis=0)) / divisor, updated)
```

```python
import functools
import math

import jax
import jax.numpy as jnp
import numpy as np
from jax import lax
from jax.experimental import pallas as pl
from jax.experimental.pallas import tpu as pltpu
from jax.sharding import Mesh, PartitionSpec as P

ROWS = 128
BLK = 4
CHUNK = 256
DP = ("zl", "x", "y")
NEAR = ("c", "zl", "x")
FAR = ("zh", "y")
F32 = jnp.float32
BF16 = jnp.bfloat16


def params(mib):
    return pltpu.CompilerParams(vmem_limit_bytes=mib * 1024 * 1024)


def adam_step(master, moment, second, gradient):
    moment_new = 0.9 * moment + 0.1 * gradient
    second_new = 0.999 * second + 0.001 * jnp.square(gradient)
    return master - 0.01 * (moment_new / (jnp.sqrt(second_new) + 1e-08) + 0.1 * master)


def write_shifts(lengths_ref, shift_ref):
    taps, height, _ = shift_ref.shape
    half = (taps - 1) // 2
    row = lax.broadcasted_iota(jnp.int32, (height, height), 0)
    col = lax.broadcasted_iota(jnp.int32, (height, height), 1)
    bound = jnp.int32(0)
    row_seg = jnp.zeros((height, height), jnp.int32)
    col_seg = jnp.zeros((height, height), jnp.int32)
    for u in range(lengths_ref.shape[0]):
        bound = bound + lengths_ref[u]
        row_seg = row_seg + jnp.where(row >= bound, 1, 0)
        col_seg = col_seg + jnp.where(col >= bound, 1, 0)
    same = (row_seg == col_seg) & (row < bound)
    offset = jnp.where(same, col - row + half, -1)
    for j in range(taps):
        shift_ref[j] = jnp.where(offset == j, 1.0, 0.0).astype(F32).astype(BF16)


def forward_kernel(lengths_ref, dest_ref, frames_ref, kernel_ref, gain_ref, slots_ref, mixed_ref, shift_ref, act_ref):
    taps, height, _ = shift_ref.shape
    columns = frames_ref.shape[1]
    write_shifts(lengths_ref, shift_ref)

    def conv(i, carry):
        at = pl.ds(pl.multiple_of(i * CHUNK, CHUNK), CHUNK)
        piece = frames_ref[:, at]
        total = jnp.zeros((height, CHUNK), F32)
        for j in range(taps):
            total = total + kernel_ref[pl.ds(j, 1), at] * jnp.dot(shift_ref[j], piece, preferred_element_type=F32)
        mixed_ref[:, at] = total
        return carry

    lax.fori_loop(0, columns // CHUNK, conv, 0)
    step = 16

    def norm(i, carry):
        at = pl.ds(pl.multiple_of(i * step, step), step)
        mixed = mixed_ref[at, :]
        center = jnp.mean(mixed, axis=1, keepdims=True)
        off = mixed - center
        spread = jnp.mean(off * off, axis=1, keepdims=True)
        scaled = off * lax.rsqrt(spread + 1e-05) * gain_ref[...]
        act_ref[at, :] = scaled * jax.nn.sigmoid(scaled)
        return carry

    lax.fori_loop(0, height // step, norm, 0)
    for b in range(height // BLK):
        where = dest_ref[b]

        @pl.when(where >= 0)
        def _():
            slots_ref[where] = act_ref[b * BLK : (b + 1) * BLK, :].astype(BF16)


def find_senders(flags_ref, table_ref):
    for k in range(table_ref.shape[0]):
        table_ref[k] = 0

    def look(s, count):
        sends = flags_ref[s] > 0

        @pl.when(sends)
        def _():
            table_ref[count] = s

        return count + jnp.where(sends, 1, 0)

    lax.fori_loop(0, flags_ref.shape[0], look, jnp.int32(0))


def scatter_kernel(flags_ref, cot_ref, slots_ref, table_ref):
    find_senders(flags_ref, table_ref)
    for k in range(cot_ref.shape[0] // BLK):
        base = k // 4 * 16
        rows = cot_ref[base : base + 16, :].astype(F32)
        low = k % 4 * BLK
        slots_ref[table_ref[k]] = rows[low : low + BLK, :].astype(BF16)


def load_weight(place_ref, own, cross, weight_ref, sems):
    size, width = own[0].shape
    part = size // 2
    core = place_ref[1]
    copies = []
    for h in range(2):
        start = core * width if h == 0 else (1 - core) * width
        at = pl.ds(pl.multiple_of(start, 128), width)
        pairs = [(own[h], 0, size), (cross[h][0], size, part), (cross[h][1], size + part, part)]
        for source, row, count in pairs:
            copies.append(
                pltpu.make_async_copy(source, weight_ref.at[pl.ds(row, count), at], sems.at[len(copies)])
            )
    for copy in copies:
        copy.start()
    return copies


def block_place(place_ref, owner, blocks):
    nx, ny = 4, blocks // 8
    other = jnp.where(owner // (ny * nx) != place_ref[0], blocks // 2, 0)
    return other + owner % ny * nx + owner // ny % nx


def backward_kernel(
    lengths_ref, dest_ref, place_ref, order_ref,
    frames_ref, kernel_ref, gain_ref, mixed_ref, slots_ref, o0, o1, c00, c01, c10, c11,
    frame_ref, term_ref,
    shift_ref, home_ref, homeb_ref, weight_ref, raw_ref, sorted_ref, grad_ref, gradb_ref, sems,
):
    taps, height, _ = shift_ref.shape
    columns = frames_ref.shape[1]
    blocks = order_ref.shape[0]
    size = columns // blocks
    copies = load_weight(place_ref, (o0, o1), ((c00, c01), (c10, c11)), weight_ref, sems)
    write_shifts(lengths_ref, shift_ref)
    for b in range(height // BLK):
        where = dest_ref[b]
        rows = slots_ref[jnp.maximum(where, 0)].astype(F32)
        home_ref[b * BLK : (b + 1) * BLK, :] = jnp.where(where >= 0, rows, 0.0)
    homeb_ref[...] = home_ref[...].astype(BF16)
    for copy in copies:
        copy.wait()

    def back(i, carry):
        at = pl.ds(pl.multiple_of(i * CHUNK, CHUNK), CHUNK)
        raw_ref[at, :] = lax.dot_general(
            weight_ref[at, :], homeb_ref[...], (((1,), (1,)), ((), ())), preferred_element_type=F32
        )
        return carry

    lax.fori_loop(0, columns // CHUNK, back, 0)

    def order(b, carry):
        at = pl.multiple_of(block_place(place_ref, order_ref[b], blocks) * size, 8)
        sorted_ref[pl.ds(pl.multiple_of(b * size, 8), size), :] = raw_ref[pl.ds(at, size), :]
        return carry

    lax.fori_loop(0, blocks, order, 0)

    def turn(i, carry):
        at = pl.ds(pl.multiple_of(i * CHUNK, CHUNK), CHUNK)
        home_ref[:, at] = sorted_ref[at, :].T.astype(BF16).astype(F32)
        return carry

    lax.fori_loop(0, columns // CHUNK, turn, 0)
    step = 8
    gain = gain_ref[...]

    def norm(i, total):
        at = pl.ds(pl.multiple_of(i * step, step), step)
        mixed = mixed_ref[at, :]
        center = jnp.mean(mixed, axis=1, keepdims=True)
        off = mixed - center
        inv = lax.rsqrt(jnp.mean(off * off, axis=1, keepdims=True) + 1e-05)
        unit = off * inv
        scaled = unit * gain
        sig = jax.nn.sigmoid(scaled)
        slope = home_ref[at, :] * (sig * (1.0 + scaled * (1.0 - sig)))
        total = total + slope * unit
        slope = slope * gain
        mean_slope = jnp.mean(slope, axis=1, keepdims=True)
        mean_unit = jnp.mean(slope * unit, axis=1, keepdims=True)
        grad_ref[at, :] = inv * (slope - mean_slope - unit * mean_unit)
        return total

    total = lax.fori_loop(0, height // step, norm, jnp.zeros((step, columns), F32))
    term_ref[taps] = jnp.sum(total, axis=0, keepdims=True)
    gradb_ref[...] = grad_ref[...].astype(BF16)

    def conv(i, carry):
        at = pl.ds(pl.multiple_of(i * CHUNK, CHUNK), CHUNK)
        piece = frames_ref[:, at]
        grad = grad_ref[:, at]
        gradb = gradb_ref[:, at]
        out = jnp.zeros((height, CHUNK), F32)
        for j in range(taps):
            moved = jnp.dot(shift_ref[j], piece, preferred_element_type=F32)
            term_ref[j, :, at] = jnp.sum(grad * moved, axis=0, keepdims=True)
            out = out + kernel_ref[pl.ds(taps - 1 - j, 1), at] * jnp.dot(shift_ref[j], gradb, preferred_element_type=F32)
        frame_ref[:, at] = out.astype(BF16)
        return carry

    lax.fori_loop(0, columns // CHUNK, conv, 0)


def project_kernel(
    flags_ref, place_ref, order_ref,
    slots_ref, o0, o1, c00, c01, c10, c11,
    out_ref,
    table_ref, rows_ref, turned_ref, weight_ref, sems,
):
    blocks = order_ref.shape[0]
    size = weight_ref.shape[0] // blocks
    copies = load_weight(place_ref, (o0, o1), ((c00, c01), (c10, c11)), weight_ref, sems)
    find_senders(flags_ref, table_ref)
    for k in range(rows_ref.shape[0] // BLK):
        rows_ref[k * BLK : (k + 1) * BLK, :] = slots_ref[table_ref[k]].astype(F32)
    turned = rows_ref[...].T
    for b in range(blocks):
        at = pl.multiple_of(block_place(place_ref, order_ref[b], blocks) * size, 8)
        turned_ref[pl.ds(at, size), :] = turned[b * size : (b + 1) * size, :]
    rows = turned_ref[...].T.astype(BF16)
    for copy in copies:
        copy.wait()
    out_ref[...] = jnp.dot(rows, weight_ref[...], preferred_element_type=F32).astype(BF16)


VM = pl.BlockSpec(memory_space=pltpu.VMEM)
SM = pl.BlockSpec(memory_space=pltpu.SMEM)
HB = pl.BlockSpec(memory_space=pl.ANY)


def call(fn, ins, outs, scratch, mib, name, flops, nbytes):
    return pl.pallas_call(
        fn,
        in_specs=ins,
        out_specs=[VM] * len(outs),
        out_shape=outs,
        scratch_shapes=scratch,
        compiler_params=params(mib),
        cost_estimate=pl.CostEstimate(flops=flops, transcendentals=0, bytes_accessed=nbytes),
        name=name,
    )


def exchange(x, axes):
    return lax.all_to_all(x, axes, split_axis=0, concat_axis=0, tiled=True)


def body(frames, lengths, destination, kernel, norm_gain, master, moment, second, gradient, bucket_order, cotangent):
    height, columns = frames.shape
    taps = kernel.shape[0]
    owners = bucket_order.shape[0]
    half = columns // 2
    core, zl = lax.axis_index("c"), lax.axis_index("zl")
    dest = destination[0]
    lens = lengths[0]
    place = jnp.stack([zl, core]).astype(jnp.int32)
    gain = norm_gain[None, :]

    sends = jnp.any(dest[None, :] == jnp.arange(owners, dtype=jnp.int32)[:, None], axis=1).astype(jnp.int32)
    flags = exchange(jnp.broadcast_to(sends[:, None, None], (owners, 1, 128)), DP)[:, 0, 0]

    updated = adam_step(master, moment, second, gradient)
    bucket = lax.dynamic_slice_in_dim(updated, core * half, half, axis=1).astype(BF16)
    near = lax.all_gather(bucket, "x", axis=0, tiled=True)
    own = lax.all_gather(near, "y", axis=0, tiled=True)
    slots = jax.ShapeDtypeStruct((owners, BLK, columns), BF16)
    sent, mixed = call(
        forward_kernel,
        [SM, SM, VM, VM, VM],
        [slots, jax.ShapeDtypeStruct((height, columns), F32)],
        [pltpu.VMEM((taps, height, height), BF16), pltpu.VMEM((height, columns), F32)],
        40,
        "forward",
        8 * taps * height * height * columns,
        16 * height * columns,
    )(lens, dest, frames, kernel, gain)

    own, sent = lax.optimization_barrier((own, sent))
    part = own.shape[0] // 2
    nz = lax.axis_size("zh") * lax.axis_size("zl")
    up = [(i, (i + 1) % nz) for i in range(nz)]
    down = [((i + 1) % nz, i) for i in range(nz)]
    swap = [(0, 1), (1, 0)]
    c00 = lax.ppermute(own[:part], ("zh", "zl"), up)
    c01 = lax.ppermute(own[part:], ("zh", "zl"), down)
    own1 = lax.ppermute(own, "c", swap)
    c10 = lax.ppermute(c00, "c", swap)
    c11 = lax.ppermute(c01, "c", swap)
    pieces = (own, own1, c00, c01, c10, c11)

    (cot_sent,) = call(
        scatter_kernel, [SM, VM], [slots], [pltpu.SMEM((owners,), jnp.int32)], 40, "scatter", 0, 6 * cotangent.size
    )(flags, cotangent)
    cot_slots = exchange(cot_sent, DP)
    sent, cot_slots = lax.optimization_barrier((sent, cot_slots))
    act_slots = exchange(sent, DP)

    frame_grad, term = call(
        backward_kernel,
        [SM] * 4 + [VM] * 5 + [HB] * 6,
        [
            jax.ShapeDtypeStruct((height, columns), BF16),
            jax.ShapeDtypeStruct((taps + 1, 1, columns), F32),
        ],
        [
            pltpu.VMEM((taps, height, height), BF16),
            pltpu.VMEM((height, columns), F32),
            pltpu.VMEM((height, columns), BF16),
            pltpu.VMEM((columns, columns), BF16),
            pltpu.VMEM((columns, height), F32),
            pltpu.VMEM((columns, height), F32),
            pltpu.VMEM((height, columns), F32),
            pltpu.VMEM((height, columns), BF16),
            pltpu.SemaphoreType.DMA((6,)),
        ],
        48,
        "backward",
        8 * taps * height * height * columns + 2 * height * columns * columns,
        16 * height * columns + 2 * columns * columns,
    )(lens, dest, place, bucket_order, frames, kernel, gain, mixed, cot_slots, *pieces)

    mine = jnp.sum(exchange(term, NEAR), axis=0, keepdims=True)
    far = lax.axis_size(FAR)
    mine = jnp.sum(exchange(jnp.broadcast_to(mine, (far, 1, columns)), FAR), axis=0, keepdims=True)
    divisor = math.sqrt(lax.axis_size(("zh", "c")) * owners * ROWS)
    sums = exchange(jnp.broadcast_to(mine / divisor, (taps + 1, 1, columns)), NEAR)[:, 0, :]

    (projected,) = call(
        project_kernel,
        [SM] * 3 + [VM] + [HB] * 6,
        [jax.ShapeDtypeStruct(cotangent.shape, BF16)],
        [
            pltpu.SMEM((owners,), jnp.int32),
            pltpu.VMEM(cotangent.shape, F32),
            pltpu.VMEM(cotangent.shape[::-1], F32),
            pltpu.VMEM((columns, columns), BF16),
            pltpu.SemaphoreType.DMA((6,)),
        ],
        40,
        "project",
        2 * cotangent.size * columns,
        4 * cotangent.size + 2 * columns * columns,
    )(flags, place, bucket_order, act_slots, *pieces)
    return projected, frame_grad, sums[:taps], sums[taps], updated


def solution(mesh):
    fine = Mesh(mesh.devices.reshape(4, 2, 2, 4, 8), ("zh", "c", "zl", "x", "y"))
    rep, dp = ("zh", "c"), ("zl", "x", "y")
    every, rows = P(rep + dp, None), P(dp, None)
    return jax.shard_map(
        body,
        mesh=fine,
        in_specs=(every, every, every, P(), P(), rows, rows, rows, rows, P(), every),
        out_specs=(every, every, P(), P(), rows),
        check_vma=False,
    )
```

```python
import math

import jax
import jax.numpy as jnp
from jax import lax
from jax.experimental import pallas as pl
from jax.experimental.pallas import tpu as pltpu
from jax.sharding import Mesh, PartitionSpec as P

ROWS = 128
BLK = 4
CHUNK = 256
EMPTY = -2.0
DP = ("zl", "x", "y")
NEAR = ("c", "zl", "x")
FAR = ("zh", "y")
NX = 4
F32 = jnp.float32
BF16 = jnp.bfloat16


def params(mib):
    return pltpu.CompilerParams(vmem_limit_bytes=mib * 1024 * 1024)


def adam_step(master, moment, second, gradient):
    moment_new = 0.9 * moment + 0.1 * gradient
    second_new = 0.999 * second + 0.001 * jnp.square(gradient)
    return master - 0.01 * (moment_new / (jnp.sqrt(second_new) + 1e-08) + 0.1 * master)


def write_shifts(lengths_ref, shift_ref, taps):
    height = shift_ref.shape[1]
    half = (taps - 1) // 2
    row = lax.broadcasted_iota(jnp.int32, (height, height), 0)
    col = lax.broadcasted_iota(jnp.int32, (height, height), 1)
    bound = jnp.int32(0)
    row_seg = jnp.zeros((height, height), jnp.int32)
    col_seg = jnp.zeros((height, height), jnp.int32)
    for u in range(lengths_ref.shape[0]):
        bound = bound + lengths_ref[u]
        row_seg = row_seg + jnp.where(row >= bound, 1, 0)
        col_seg = col_seg + jnp.where(col >= bound, 1, 0)
    same = (row_seg == col_seg) & (row < bound)
    offset = jnp.where(same, col - row + half, -1)
    for j in range(taps):
        shift_ref[j * height : (j + 1) * height, :] = jnp.where(offset == j, 1.0, 0.0).astype(F32).astype(BF16)


def forward_kernel(
    lengths_ref, dest_ref, frames_ref, kernel_ref, gain_ref,
    slots_ref, unit_ref, factor_ref, inv_ref, shift_ref,
    act_ref,
):
    taps = kernel_ref.shape[0]
    height, columns = frames_ref.shape
    write_shifts(lengths_ref, shift_ref, taps)

    def conv(i, carry):
        at = pl.ds(pl.multiple_of(i * CHUNK, CHUNK), CHUNK)
        piece = frames_ref[:, at]
        total = jnp.zeros((height, CHUNK), F32)
        for j in range(taps):
            moved = jnp.dot(shift_ref[j * height : (j + 1) * height, :], piece, preferred_element_type=F32)
            total = total + kernel_ref[pl.ds(j, 1), at] * moved
        act_ref[:, at] = total
        return carry

    lax.fori_loop(0, columns // CHUNK, conv, 0)
    step = 16
    gain = gain_ref[...]

    def norm(i, carry):
        at = pl.ds(pl.multiple_of(i * step, step), step)
        mixed = act_ref[at, :]
        center = jnp.mean(mixed, axis=1, keepdims=True)
        off = mixed - center
        inv = lax.rsqrt(jnp.mean(off * off, axis=1, keepdims=True) + 1e-05)
        unit = off * inv
        scaled = unit * gain
        sig = jax.nn.sigmoid(scaled)
        act = scaled * sig
        act_ref[at, :] = act
        unit_ref[at, :] = unit
        factor_ref[at, :] = sig + act * (1.0 - sig)
        inv_ref[at, :] = jnp.broadcast_to(inv, (step, inv_ref.shape[1]))
        return carry

    lax.fori_loop(0, height // step, norm, 0)
    slots_ref[:, :, 0:128] = jnp.full((slots_ref.shape[0], BLK, 128), EMPTY, BF16)
    for b in range(height // BLK):
        where = dest_ref[b]

        @pl.when(where >= 0)
        def _():
            slots_ref[where] = act_ref[b * BLK : (b + 1) * BLK, :].astype(BF16)


def find_senders(flags_ref, table_ref):
    for k in range(table_ref.shape[0]):
        table_ref[k] = 0

    def look(s, count):
        sends = flags_ref[s] > 0

        @pl.when(sends)
        def _():
            table_ref[count] = s

        return count + jnp.where(sends, 1, 0)

    lax.fori_loop(0, flags_ref.shape[0], look, jnp.int32(0))


def scatter_kernel(flags_ref, cot_ref, slots_ref, table_ref):
    find_senders(flags_ref, table_ref)
    for k in range(cot_ref.shape[0] // BLK):
        base = k // 4 * 16
        rows = cot_ref[base : base + 16, :].astype(F32)
        low = k % 4 * BLK
        slots_ref[table_ref[k]] = rows[low : low + BLK, :].astype(BF16)


def load_weight(place_ref, own, cross, weight_ref, sems):
    size, width = own[0].shape
    part = size // 2
    core = place_ref[1]
    copies = []
    for h in range(2):
        start = core * width if h == 0 else (1 - core) * width
        at = pl.ds(pl.multiple_of(start, 128), width)
        pairs = [(own[h], 0, size), (cross[h][0], size, part), (cross[h][1], size + part, part)]
        for source, row, count in pairs:
            copies.append(
                pltpu.make_async_copy(source, weight_ref.at[pl.ds(row, count), at], sems.at[len(copies)])
            )
    for copy in copies:
        copy.start()
    return copies


def block_place(place_ref, owner, blocks):
    nx, ny = NX, blocks // (2 * NX)
    other = jnp.where(owner // (ny * nx) != place_ref[0], blocks // 2, 0)
    return other + (owner // ny % nx - place_ref[2] + nx) % nx * ny + owner % ny


def backward_kernel(
    dest_ref, place_ref, order_ref,
    frames_ref, kernel_ref, gain_ref, unit_ref, factor_ref, inv_ref, shift_ref, slots_ref,
    o0, o1, c00, c01, c10, c11,
    frame_ref, term_ref,
    home_ref, homeb_ref, weight_ref, raw_ref, sorted_ref, grad_ref, moved_ref, sum_ref, sems,
):
    taps = kernel_ref.shape[0]
    height, columns = frames_ref.shape
    blocks = order_ref.shape[0]
    size = columns // blocks
    copies = load_weight(place_ref, (o0, o1), ((c00, c01), (c10, c11)), weight_ref, sems)
    for b in range(height // BLK):
        where = dest_ref[b]
        rows = slots_ref[jnp.maximum(where, 0)].astype(F32)
        home_ref[b * BLK : (b + 1) * BLK, :] = jnp.where(where >= 0, rows, 0.0)
    homeb_ref[...] = home_ref[...].astype(BF16)
    for copy in copies:
        copy.wait()

    def back(i, carry):
        at = pl.ds(pl.multiple_of(i * 2 * CHUNK, CHUNK), 2 * CHUNK)
        raw_ref[at, :] = lax.dot_general(
            weight_ref[at, :], homeb_ref[...], (((1,), (1,)), ((), ())), preferred_element_type=F32
        )
        return carry

    lax.fori_loop(0, columns // (2 * CHUNK), back, 0)
    for b in range(blocks):
        at = pl.multiple_of(block_place(place_ref, order_ref[b], blocks) * size, 8)
        sorted_ref[b * size : (b + 1) * size, :] = raw_ref[pl.ds(at, size), :]

    def turn(i, carry):
        at = pl.ds(pl.multiple_of(i * CHUNK, CHUNK), CHUNK)
        home_ref[:, at] = sorted_ref[at, :].T.astype(BF16).astype(F32)
        return carry

    lax.fori_loop(0, columns // CHUNK, turn, 0)
    step = 16
    gain = gain_ref[...]

    def norm(i, total):
        at = pl.ds(pl.multiple_of(i * step, step), step)
        unit = unit_ref[at, :]
        slope = home_ref[at, :] * factor_ref[at, :]
        along = slope * unit
        total = total + along[0:8] + along[8:16]
        slope = slope * gain
        mean_slope = jnp.mean(slope, axis=1, keepdims=True)
        mean_unit = jnp.mean(along * gain, axis=1, keepdims=True)
        grad_ref[at, :] = (inv_ref[at, 0:1] * (slope - mean_slope - unit * mean_unit)).astype(BF16)
        return total

    total = lax.fori_loop(0, height // step, norm, jnp.zeros((8, columns), F32))
    term_ref[taps] = jnp.sum(total, axis=0, keepdims=True)
    part = 64

    def conv(i, carry):
        at = pl.ds(pl.multiple_of(i * CHUNK, CHUNK), CHUNK)
        moved_ref[...] = jnp.dot(shift_ref[...], grad_ref[:, at], preferred_element_type=F32)
        for p in range(height // part):
            rows = slice(p * part, (p + 1) * part)
            frames = frames_ref[rows, at].astype(F32)
            out = jnp.zeros((part, CHUNK), F32)
            for j in range(taps):
                tap = taps - 1 - j
                moved = moved_ref[j * height + p * part : j * height + (p + 1) * part, :]
                out = out + kernel_ref[pl.ds(tap, 1), at] * moved
                add = jnp.sum((frames * moved).reshape(part // 8, 8, CHUNK), axis=0)
                if p == 0:
                    sum_ref[tap] = add
                elif p < height // part - 1:
                    sum_ref[tap] = sum_ref[tap] + add
                else:
                    term_ref[tap, :, at] = jnp.sum(sum_ref[tap] + add, axis=0, keepdims=True)
            frame_ref[rows, at] = out.astype(BF16)
        return carry

    lax.fori_loop(0, columns // CHUNK, conv, 0)


def project_kernel(
    flags_ref, place_ref, order_ref,
    slots_ref, o0, o1, c00, c01, c10, c11,
    out_ref,
    table_ref, rows_ref, turned_ref, weight_ref, sems,
):
    blocks = order_ref.shape[0]
    size = weight_ref.shape[0] // blocks
    copies = load_weight(place_ref, (o0, o1), ((c00, c01), (c10, c11)), weight_ref, sems)
    find_senders(flags_ref, table_ref)
    for k in range(rows_ref.shape[0] // BLK):
        rows_ref[k * BLK : (k + 1) * BLK, :] = slots_ref[table_ref[k]].astype(F32)
    turned = rows_ref[...].T
    for b in range(blocks):
        at = pl.multiple_of(block_place(place_ref, order_ref[b], blocks) * size, 8)
        turned_ref[pl.ds(at, size), :] = turned[b * size : (b + 1) * size, :]
    rows = turned_ref[...].T.astype(BF16)
    for copy in copies:
        copy.wait()
    out_ref[...] = jnp.dot(rows, weight_ref[...], preferred_element_type=F32).astype(BF16)


VM = pl.BlockSpec(memory_space=pltpu.VMEM)
SM = pl.BlockSpec(memory_space=pltpu.SMEM)
HB = pl.BlockSpec(memory_space=pl.ANY)


def call(fn, ins, outs, scratch, mib, name, flops, nbytes):
    return pl.pallas_call(
        fn,
        in_specs=ins,
        out_specs=[VM] * len(outs),
        out_shape=outs,
        scratch_shapes=scratch,
        compiler_params=params(mib),
        cost_estimate=pl.CostEstimate(flops=flops, transcendentals=0, bytes_accessed=nbytes),
        name=name,
    )


def exchange(x, axes):
    return lax.all_to_all(x, axes, split_axis=0, concat_axis=0, tiled=True)


def body(frames, lengths, destination, kernel, norm_gain, master, moment, second, gradient, bucket_order, cotangent):
    height, columns = frames.shape
    taps = kernel.shape[0]
    owners = bucket_order.shape[0]
    half = columns // 2
    core, zl, x = lax.axis_index("c"), lax.axis_index("zl"), lax.axis_index("x")
    dest = destination[0]
    lens = lengths[0]
    place = jnp.stack([zl, core, x]).astype(jnp.int32)
    gain = norm_gain[None, :]

    updated = adam_step(master, moment, second, gradient)
    bucket = lax.dynamic_slice_in_dim(updated, core * half, half, axis=1).astype(BF16)
    ny = lax.axis_size("y")
    line = exchange(jnp.broadcast_to(bucket[None], (ny, *bucket.shape)), "y").reshape(-1, half)

    slots = jax.ShapeDtypeStruct((owners, BLK, columns), BF16)
    whole = jax.ShapeDtypeStruct((height, columns), F32)
    sent, unit, factor, inv, shifts = call(
        forward_kernel,
        [SM, SM, VM, VM, VM],
        [
            slots,
            whole,
            whole,
            jax.ShapeDtypeStruct((height, 128), F32),
            jax.ShapeDtypeStruct((taps * height, height), BF16),
        ],
        [pltpu.VMEM((height, columns), F32)],
        40,
        "forward",
        8 * taps * height * height * columns,
        16 * height * columns,
    )(lens, dest, frames, kernel, gain)
    line, sent = lax.optimization_barrier((line, sent))
    act_slots = exchange(sent, DP)

    nx = lax.axis_size("x")
    by_x = [line] + [lax.ppermute(line, "x", [((i + k) % nx, i) for i in range(nx)]) for k in range(1, nx)]
    nz = lax.axis_size("zh") * lax.axis_size("zl")
    up = [(i, (i + 1) % nz) for i in range(nz)]
    down = [((i + 1) % nz, i) for i in range(nz)]
    swap = [(0, 1), (1, 0)]
    low, high = jnp.concatenate(by_x[: nx // 2]), jnp.concatenate(by_x[nx // 2 :])
    c00 = lax.ppermute(low, ("zh", "zl"), up)
    c01 = lax.ppermute(high, ("zh", "zl"), down)
    own = jnp.concatenate(by_x)
    own1 = lax.ppermute(own, "c", swap)
    c10 = lax.ppermute(c00, "c", swap)
    c11 = lax.ppermute(c01, "c", swap)
    pieces = (own, own1, c00, c01, c10, c11)

    flags = (act_slots[:, 0, 0] > EMPTY / 2).astype(jnp.int32)
    (cot_sent,) = call(
        scatter_kernel, [SM, VM], [slots], [pltpu.SMEM((owners,), jnp.int32)], 40, "scatter", 0, 6 * cotangent.size
    )(flags, cotangent)
    cot_slots = exchange(cot_sent, DP)

    frame_grad, term = call(
        backward_kernel,
        [SM] * 3 + [VM] * 8 + [HB] * 6,
        [
            jax.ShapeDtypeStruct((height, columns), BF16),
            jax.ShapeDtypeStruct((taps + 1, 1, columns), F32),
        ],
        [
            pltpu.VMEM((height, columns), F32),
            pltpu.VMEM((height, columns), BF16),
            pltpu.VMEM((columns, columns), BF16),
            pltpu.VMEM((columns, height), F32),
            pltpu.VMEM((columns, height), F32),
            pltpu.VMEM((height, columns), BF16),
            pltpu.VMEM((taps * height, CHUNK), F32),
            pltpu.VMEM((taps, 8, CHUNK), F32),
            pltpu.SemaphoreType.DMA((6,)),
        ],
        48,
        "backward",
        8 * taps * height * height * columns + 2 * height * columns * columns,
        16 * height * columns + 2 * columns * columns,
    )(dest, place, bucket_order, frames, kernel, gain, unit, factor, inv, shifts, cot_slots, *pieces)

    mine = jnp.sum(exchange(term, NEAR), axis=0, keepdims=True)
    far = lax.axis_size(FAR)
    mine = jnp.sum(exchange(jnp.broadcast_to(mine, (far, 1, columns)), FAR), axis=0, keepdims=True)
    divisor = math.sqrt(lax.axis_size(("zh", "c")) * owners * ROWS)
    sums = exchange(jnp.broadcast_to(mine / divisor, (taps + 1, 1, columns)), NEAR)[:, 0, :]

    (projected,) = call(
        project_kernel,
        [SM] * 3 + [VM] + [HB] * 6,
        [jax.ShapeDtypeStruct(cotangent.shape, BF16)],
        [
            pltpu.SMEM((owners,), jnp.int32),
            pltpu.VMEM(cotangent.shape, F32),
            pltpu.VMEM(cotangent.shape[::-1], F32),
            pltpu.VMEM((columns, columns), BF16),
            pltpu.SemaphoreType.DMA((6,)),
        ],
        40,
        "project",
        2 * cotangent.size * columns,
        4 * cotangent.size + 2 * columns * columns,
    )(flags, place, bucket_order, act_slots, *pieces)
    return projected, frame_grad, sums[:taps], sums[taps], updated


def solution(mesh):
    fine = Mesh(mesh.devices.reshape(4, 2, 2, NX, 8), ("zh", "c", "zl", "x", "y"))
    rep, dp = ("zh", "c"), ("zl", "x", "y")
    every, rows = P(rep + dp, None), P(dp, None)
    return jax.shard_map(
        body,
        mesh=fine,
        in_specs=(every, every, every, P(), P(), rows, rows, rows, rows, P(), every),
        out_specs=(every, every, P(), P(), rows),
        check_vma=False,
    )
```

```python
import math

import jax
import jax.numpy as jnp
from jax import lax
from jax.experimental import pallas as pl
from jax.experimental.pallas import tpu as pltpu
from jax.sharding import Mesh, PartitionSpec as P

ROWS = 128
BLK = 4
CHUNK = 256
DP = ("zl", "x", "y")
NEAR = ("c", "zl", "x")
FAR = ("zh", "y")
NX = 4
F32 = jnp.float32
BF16 = jnp.bfloat16


def params(mib):
    return pltpu.CompilerParams(vmem_limit_bytes=mib * 1024 * 1024)


def adam_step(master, moment, second, gradient):
    moment_new = 0.9 * moment + 0.1 * gradient
    second_new = 0.999 * second + 0.001 * jnp.square(gradient)
    return master - 0.01 * (moment_new / (jnp.sqrt(second_new) + 1e-08) + 0.1 * master)


def write_shifts(lengths_ref, shift_ref, taps):
    height = shift_ref.shape[1]
    half = (taps - 1) // 2
    row = lax.broadcasted_iota(jnp.int32, (height, height), 0)
    col = lax.broadcasted_iota(jnp.int32, (height, height), 1)
    bound = jnp.int32(0)
    row_seg = jnp.zeros((height, height), jnp.int32)
    col_seg = jnp.zeros((height, height), jnp.int32)
    for u in range(lengths_ref.shape[0]):
        bound = bound + lengths_ref[u]
        row_seg = row_seg + jnp.where(row >= bound, 1, 0)
        col_seg = col_seg + jnp.where(col >= bound, 1, 0)
    same = (row_seg == col_seg) & (row < bound)
    offset = jnp.where(same, col - row + half, -1)
    for j in range(taps):
        shift_ref[j * height : (j + 1) * height, :] = jnp.where(offset == j, 1.0, 0.0).astype(F32).astype(BF16)


def forward_kernel(
    lengths_ref, dest_ref, frames_ref, kernel_ref, gain_ref,
    slots_ref, inv_ref, unit_hbm, factor_hbm, shift_hbm,
    unit_ref, factor_ref, shift_ref, act_ref, sems,
):
    taps = kernel_ref.shape[0]
    height, columns = frames_ref.shape
    write_shifts(lengths_ref, shift_ref, taps)
    saved = [(shift_ref, shift_hbm), (unit_ref, unit_hbm), (factor_ref, factor_hbm)]
    copies = [pltpu.make_async_copy(a, b, sems.at[i]) for i, (a, b) in enumerate(saved)]
    copies[0].start()

    def conv(i, carry):
        at = pl.ds(pl.multiple_of(i * CHUNK, CHUNK), CHUNK)
        piece = frames_ref[:, at]
        total = jnp.zeros((height, CHUNK), F32)
        for j in range(taps):
            moved = jnp.dot(shift_ref[j * height : (j + 1) * height, :], piece, preferred_element_type=F32)
            total = total + kernel_ref[pl.ds(j, 1), at] * moved
        act_ref[:, at] = total
        return carry

    lax.fori_loop(0, columns // CHUNK, conv, 0)
    step = 16
    gain = gain_ref[...]

    def norm(i, carry):
        at = pl.ds(pl.multiple_of(i * step, step), step)
        mixed = act_ref[at, :]
        center = jnp.mean(mixed, axis=1, keepdims=True)
        off = mixed - center
        inv = lax.rsqrt(jnp.mean(off * off, axis=1, keepdims=True) + 1e-05)
        unit = off * inv
        scaled = unit * gain
        sig = jax.nn.sigmoid(scaled)
        act = scaled * sig
        act_ref[at, :] = act
        unit_ref[at, :] = unit
        factor_ref[at, :] = sig + act * (1.0 - sig)
        inv_ref[at, :] = jnp.broadcast_to(inv, (step, inv_ref.shape[1]))
        return carry

    lax.fori_loop(0, height // step, norm, 0)
    copies[1].start()
    copies[2].start()
    for b in range(height // BLK):
        where = dest_ref[b]

        @pl.when(where >= 0)
        def _():
            slots_ref[where, 0:BLK, :] = act_ref[b * BLK : (b + 1) * BLK, :].astype(BF16)

    for copy in copies:
        copy.wait()


def find_senders(flags_ref, table_ref):
    for k in range(table_ref.shape[0]):
        table_ref[k] = 0

    def look(s, count):
        sends = flags_ref[s] > 0

        @pl.when(sends)
        def _():
            table_ref[count] = s

        return count + jnp.where(sends, 1, 0)

    lax.fori_loop(0, flags_ref.shape[0], look, jnp.int32(0))


def pack_kernel(flags_ref, cot_ref, act_ref, slots_ref, table_ref):
    find_senders(flags_ref, table_ref)
    slots_ref[...] = act_ref[...]
    for k in range(cot_ref.shape[0] // BLK):
        base = k // 4 * 16
        rows = cot_ref[base : base + 16, :].astype(F32)
        low = k % 4 * BLK
        slots_ref[table_ref[k], BLK : 2 * BLK, :] = rows[low : low + BLK, :].astype(BF16)


def load_weight(place_ref, own, cross, weight_ref, sems):
    size, width = own[0].shape
    part = size // 2
    core = place_ref[1]
    copies = []
    for h in range(2):
        start = core * width if h == 0 else (1 - core) * width
        at = pl.ds(pl.multiple_of(start, 128), width)
        pairs = [(own[h], 0, size), (cross[h][0], size, part), (cross[h][1], size + part, part)]
        for source, row, count in pairs:
            copies.append(
                pltpu.make_async_copy(source, weight_ref.at[pl.ds(row, count), at], sems.at[len(copies)])
            )
    for copy in copies:
        copy.start()
    return copies


def block_place(place_ref, owner, blocks):
    nx, ny = NX, blocks // (2 * NX)
    other = jnp.where(owner // (ny * nx) != place_ref[0], blocks // 2, 0)
    return other + (owner // ny % nx - place_ref[2] + nx) % nx * ny + owner % ny


def backward_kernel(
    dest_ref, place_ref, order_ref,
    kernel_ref, gain_ref, inv_ref, slots_ref,
    frames_hbm, unit_hbm, factor_hbm, shift_hbm, o0, o1, c00, c01, c10, c11,
    frame_ref, term_ref,
    frames_ref, unit_ref, factor_ref, shift_ref,
    home_ref, homeb_ref, weight_ref, raw_ref, sorted_ref, grad_ref, moved_ref, sum_ref, sems,
):
    taps = kernel_ref.shape[0]
    height, columns = frames_ref.shape
    blocks = order_ref.shape[0]
    size = columns // blocks
    copies = load_weight(place_ref, (o0, o1), ((c00, c01), (c10, c11)), weight_ref, sems)
    saved = [(unit_hbm, unit_ref), (factor_hbm, factor_ref), (shift_hbm, shift_ref), (frames_hbm, frames_ref)]
    late = [pltpu.make_async_copy(a, b, sems.at[len(copies) + i]) for i, (a, b) in enumerate(saved)]
    for copy in late:
        copy.start()
    for b in range(height // BLK):
        where = dest_ref[b]
        rows = slots_ref[jnp.maximum(where, 0), BLK : 2 * BLK, :].astype(F32)
        home_ref[b * BLK : (b + 1) * BLK, :] = jnp.where(where >= 0, rows, 0.0)
    homeb_ref[...] = home_ref[...].astype(BF16)
    for copy in copies:
        copy.wait()

    def back(i, carry):
        at = pl.ds(pl.multiple_of(i * 2 * CHUNK, CHUNK), 2 * CHUNK)
        raw_ref[at, :] = lax.dot_general(
            weight_ref[at, :], homeb_ref[...], (((1,), (1,)), ((), ())), preferred_element_type=F32
        )
        return carry

    lax.fori_loop(0, columns // (2 * CHUNK), back, 0)
    for b in range(blocks):
        at = pl.multiple_of(block_place(place_ref, order_ref[b], blocks) * size, 8)
        sorted_ref[b * size : (b + 1) * size, :] = raw_ref[pl.ds(at, size), :]

    def turn(i, carry):
        at = pl.ds(pl.multiple_of(i * CHUNK, CHUNK), CHUNK)
        home_ref[:, at] = sorted_ref[at, :].T.astype(BF16).astype(F32)
        return carry

    lax.fori_loop(0, columns // CHUNK, turn, 0)
    for copy in late:
        copy.wait()
    step = 16
    gain = gain_ref[...]

    def norm(i, total):
        at = pl.ds(pl.multiple_of(i * step, step), step)
        unit = unit_ref[at, :]
        slope = home_ref[at, :] * factor_ref[at, :]
        along = slope * unit
        total = total + along[0:8] + along[8:16]
        slope = slope * gain
        mean_slope = jnp.mean(slope, axis=1, keepdims=True)
        mean_unit = jnp.mean(along * gain, axis=1, keepdims=True)
        grad_ref[at, :] = (inv_ref[at, 0:1] * (slope - mean_slope - unit * mean_unit)).astype(BF16)
        return total

    total = lax.fori_loop(0, height // step, norm, jnp.zeros((8, columns), F32))
    term_ref[taps] = jnp.sum(total, axis=0, keepdims=True)
    part = 64

    def conv(i, carry):
        at = pl.ds(pl.multiple_of(i * CHUNK, CHUNK), CHUNK)
        moved_ref[...] = jnp.dot(shift_ref[...], grad_ref[:, at], preferred_element_type=F32)
        for p in range(height // part):
            rows = slice(p * part, (p + 1) * part)
            frames = frames_ref[rows, at].astype(F32)
            out = jnp.zeros((part, CHUNK), F32)
            for j in range(taps):
                tap = taps - 1 - j
                moved = moved_ref[j * height + p * part : j * height + (p + 1) * part, :]
                out = out + kernel_ref[pl.ds(tap, 1), at] * moved
                add = jnp.sum((frames * moved).reshape(part // 8, 8, CHUNK), axis=0)
                if p == 0:
                    sum_ref[tap] = add
                elif p < height // part - 1:
                    sum_ref[tap] = sum_ref[tap] + add
                else:
                    term_ref[tap, :, at] = jnp.sum(sum_ref[tap] + add, axis=0, keepdims=True)
            frame_ref[rows, at] = out.astype(BF16)
        return carry

    lax.fori_loop(0, columns // CHUNK, conv, 0)


def project_kernel(
    flags_ref, place_ref, order_ref,
    slots_ref, o0, o1, c00, c01, c10, c11,
    out_ref,
    table_ref, rows_ref, turned_ref, weight_ref, sems,
):
    blocks = order_ref.shape[0]
    size = weight_ref.shape[0] // blocks
    copies = load_weight(place_ref, (o0, o1), ((c00, c01), (c10, c11)), weight_ref, sems)
    find_senders(flags_ref, table_ref)
    for k in range(rows_ref.shape[0] // BLK):
        rows_ref[k * BLK : (k + 1) * BLK, :] = slots_ref[table_ref[k], 0:BLK, :].astype(F32)
    turned = rows_ref[...].T
    for b in range(blocks):
        at = pl.multiple_of(block_place(place_ref, order_ref[b], blocks) * size, 8)
        turned_ref[pl.ds(at, size), :] = turned[b * size : (b + 1) * size, :]
    rows = turned_ref[...].T.astype(BF16)
    for copy in copies:
        copy.wait()
    out_ref[...] = jnp.dot(rows, weight_ref[...], preferred_element_type=F32).astype(BF16)


VM = pl.BlockSpec(memory_space=pltpu.VMEM)
SM = pl.BlockSpec(memory_space=pltpu.SMEM)
AN = pl.BlockSpec(memory_space=pl.ANY)
HB = pl.BlockSpec(memory_space=pltpu.HBM)


def call(fn, ins, outs, scratch, mib, name, flops, nbytes, out_specs=None):
    return pl.pallas_call(
        fn,
        in_specs=ins,
        out_specs=out_specs or [VM] * len(outs),
        out_shape=outs,
        scratch_shapes=scratch,
        compiler_params=params(mib),
        cost_estimate=pl.CostEstimate(flops=flops, transcendentals=0, bytes_accessed=nbytes),
        name=name,
    )


def exchange(x, axes):
    return lax.all_to_all(x, axes, split_axis=0, concat_axis=0, tiled=True)


def body(frames, lengths, destination, kernel, norm_gain, master, moment, second, gradient, bucket_order, cotangent):
    height, columns = frames.shape
    taps = kernel.shape[0]
    owners = bucket_order.shape[0]
    half = columns // 2
    core, zl, x = lax.axis_index("c"), lax.axis_index("zl"), lax.axis_index("x")
    dest = destination[0]
    lens = lengths[0]
    place = jnp.stack([zl, core, x]).astype(jnp.int32)
    gain = norm_gain[None, :]

    updated = adam_step(master, moment, second, gradient)
    bucket = lax.dynamic_slice_in_dim(updated, core * half, half, axis=1).astype(BF16)
    ny = lax.axis_size("y")
    line = exchange(jnp.broadcast_to(bucket[None], (ny, *bucket.shape)), "y").reshape(-1, half)

    slots = jax.ShapeDtypeStruct((owners, 2 * BLK, columns), BF16)
    whole = jax.ShapeDtypeStruct((height, columns), F32)
    shifts = jax.ShapeDtypeStruct((taps * height, height), BF16)
    sent, inv, unit, factor, shifts = call(
        forward_kernel,
        [SM, SM, VM, VM, VM],
        [slots, jax.ShapeDtypeStruct((height, 128), F32), whole, whole, shifts],
        [
            pltpu.VMEM(whole.shape, F32),
            pltpu.VMEM(whole.shape, F32),
            pltpu.VMEM(shifts.shape, BF16),
            pltpu.VMEM(whole.shape, F32),
            pltpu.SemaphoreType.DMA((3,)),
        ],
        60,
        "forward",
        8 * taps * height * height * columns,
        16 * height * columns,
        [VM] * 2 + [HB] * 3,
    )(lens, dest, frames, kernel, gain)
    sends = jnp.any(dest[None, :] == jnp.arange(owners, dtype=jnp.int32)[:, None], axis=1).astype(jnp.int32)
    sends = jnp.broadcast_to(sends[:, None, None], (owners, 1, 128))
    line, sent, sends = lax.optimization_barrier((line, sent, sends))

    nx = lax.axis_size("x")
    by_x = [line] + [lax.ppermute(line, "x", [((i + k) % nx, i) for i in range(nx)]) for k in range(1, nx)]
    flags = exchange(sends, DP)[:, 0, 0]
    nz = lax.axis_size("zh") * lax.axis_size("zl")
    up = [(i, (i + 1) % nz) for i in range(nz)]
    down = [((i + 1) % nz, i) for i in range(nz)]
    swap = [(0, 1), (1, 0)]
    low, high = jnp.concatenate(by_x[: nx // 2]), jnp.concatenate(by_x[nx // 2 :])
    own = jnp.concatenate(by_x)
    low, high, own, flags = lax.optimization_barrier((low, high, own, flags))
    c00 = lax.ppermute(low, ("zh", "zl"), up)
    c01 = lax.ppermute(high, ("zh", "zl"), down)
    own1 = lax.ppermute(own, "c", swap)
    c10 = lax.ppermute(c00, "c", swap)
    c11 = lax.ppermute(c01, "c", swap)

    (packed,) = call(
        pack_kernel, [SM, VM, VM], [slots], [pltpu.SMEM((owners,), jnp.int32)], 60, "pack", 0, 10 * cotangent.size
    )(flags, cotangent, sent)
    both_slots = exchange(packed, DP)

    pieces = (own, own1, c00, c01, c10, c11)
    frame_grad, term = call(
        backward_kernel,
        [SM] * 3 + [VM] * 4 + [HB] * 4 + [AN] * 6,
        [
            jax.ShapeDtypeStruct((height, columns), BF16),
            jax.ShapeDtypeStruct((taps + 1, 1, columns), F32),
        ],
        [
            pltpu.VMEM((height, columns), BF16),
            pltpu.VMEM((height, columns), F32),
            pltpu.VMEM((height, columns), F32),
            pltpu.VMEM(shifts.shape, BF16),
            pltpu.VMEM((height, columns), F32),
            pltpu.VMEM((height, columns), BF16),
            pltpu.VMEM((columns, columns), BF16),
            pltpu.VMEM((columns, height), F32),
            pltpu.VMEM((columns, height), F32),
            pltpu.VMEM((height, columns), BF16),
            pltpu.VMEM((taps * height, CHUNK), F32),
            pltpu.VMEM((taps, 8, CHUNK), F32),
            pltpu.SemaphoreType.DMA((10,)),
        ],
        60,
        "backward",
        8 * taps * height * height * columns + 2 * height * columns * columns,
        16 * height * columns + 2 * columns * columns,
    )(dest, place, bucket_order, kernel, gain, inv, both_slots, frames, unit, factor, shifts, *pieces)

    mine = jnp.sum(exchange(term, NEAR), axis=0, keepdims=True)
    far = lax.axis_size(FAR)
    mine = jnp.sum(exchange(jnp.broadcast_to(mine, (far, 1, columns)), FAR), axis=0, keepdims=True)
    divisor = math.sqrt(lax.axis_size(("zh", "c")) * owners * ROWS)
    sums = exchange(jnp.broadcast_to(mine / divisor, (taps + 1, 1, columns)), NEAR)[:, 0, :]

    (projected,) = call(
        project_kernel,
        [SM] * 3 + [VM] + [AN] * 6,
        [jax.ShapeDtypeStruct(cotangent.shape, BF16)],
        [
            pltpu.SMEM((owners,), jnp.int32),
            pltpu.VMEM(cotangent.shape, F32),
            pltpu.VMEM(cotangent.shape[::-1], F32),
            pltpu.VMEM((columns, columns), BF16),
            pltpu.SemaphoreType.DMA((6,)),
        ],
        60,
        "project",
        2 * cotangent.size * columns,
        4 * cotangent.size + 2 * columns * columns,
    )(flags, place, bucket_order, both_slots, *pieces)
    return projected, frame_grad, sums[:taps], sums[taps], updated


def solution(mesh):
    fine = Mesh(mesh.devices.reshape(4, 2, 2, NX, 8), ("zh", "c", "zl", "x", "y"))
    rep, dp = ("zh", "c"), ("zl", "x", "y")
    every, rows = P(rep + dp, None), P(dp, None)
    return jax.shard_map(
        body,
        mesh=fine,
        in_specs=(every, every, every, P(), P(), rows, rows, rows, rows, P(), every),
        out_specs=(every, every, P(), P(), rows),
        check_vma=False,
    )
```

```python
import math

import jax
import jax.numpy as jnp
from jax import lax
from jax.experimental import pallas as pl
from jax.experimental.pallas import tpu as pltpu
from jax.sharding import Mesh, PartitionSpec as P

ROWS = 128
BLK = 4
CHUNK = 256
EMPTY = -2.0
DP = ("zl", "x", "y")
NEAR = ("c", "zl", "x")
FAR = ("zh", "y")
NX = 4
F32 = jnp.float32
BF16 = jnp.bfloat16


def params(mib):
    return pltpu.CompilerParams(vmem_limit_bytes=mib * 1024 * 1024)


def adam_step(master, moment, second, gradient):
    moment_new = 0.9 * moment + 0.1 * gradient
    second_new = 0.999 * second + 0.001 * jnp.square(gradient)
    return master - 0.01 * (moment_new / (jnp.sqrt(second_new) + 1e-08) + 0.1 * master)


def write_shifts(lengths_ref, shift_ref, taps):
    height = shift_ref.shape[1]
    half = (taps - 1) // 2
    row = lax.broadcasted_iota(jnp.int32, (height, height), 0)
    col = lax.broadcasted_iota(jnp.int32, (height, height), 1)
    bound = jnp.int32(0)
    row_seg = jnp.zeros((height, height), jnp.int32)
    col_seg = jnp.zeros((height, height), jnp.int32)
    for u in range(lengths_ref.shape[0]):
        bound = bound + lengths_ref[u]
        row_seg = row_seg + jnp.where(row >= bound, 1, 0)
        col_seg = col_seg + jnp.where(col >= bound, 1, 0)
    same = (row_seg == col_seg) & (row < bound)
    offset = jnp.where(same, col - row + half, -1)
    for j in range(taps):
        shift_ref[j * height : (j + 1) * height, :] = jnp.where(offset == j, 1.0, 0.0).astype(F32).astype(BF16)


def forward_kernel(
    lengths_ref, dest_ref, frames_ref, kernel_ref, gain_ref,
    slots_ref, inv_ref, unit_hbm, factor_hbm, shift_hbm,
    unit_ref, factor_ref, shift_ref, act_ref, sems,
):
    taps = kernel_ref.shape[0]
    height, columns = frames_ref.shape
    write_shifts(lengths_ref, shift_ref, taps)
    saved = [(shift_ref, shift_hbm), (unit_ref, unit_hbm), (factor_ref, factor_hbm)]
    copies = [pltpu.make_async_copy(a, b, sems.at[i]) for i, (a, b) in enumerate(saved)]
    copies[0].start()

    def conv(i, carry):
        at = pl.ds(pl.multiple_of(i * CHUNK, CHUNK), CHUNK)
        piece = frames_ref[:, at]
        total = jnp.zeros((height, CHUNK), F32)
        for j in range(taps):
            moved = jnp.dot(shift_ref[j * height : (j + 1) * height, :], piece, preferred_element_type=F32)
            total = total + kernel_ref[pl.ds(j, 1), at] * moved
        act_ref[:, at] = total
        return carry

    lax.fori_loop(0, columns // CHUNK, conv, 0)
    step = 16
    gain = gain_ref[...]

    def norm(i, carry):
        at = pl.ds(pl.multiple_of(i * step, step), step)
        mixed = act_ref[at, :]
        center = jnp.mean(mixed, axis=1, keepdims=True)
        off = mixed - center
        inv = lax.rsqrt(jnp.mean(off * off, axis=1, keepdims=True) + 1e-05)
        unit = off * inv
        scaled = unit * gain
        sig = jax.nn.sigmoid(scaled)
        act = scaled * sig
        act_ref[at, :] = act
        unit_ref[at, :] = unit
        factor_ref[at, :] = sig + act * (1.0 - sig)
        inv_ref[at, :] = jnp.broadcast_to(inv, (step, inv_ref.shape[1]))
        return carry

    lax.fori_loop(0, height // step, norm, 0)
    copies[1].start()
    copies[2].start()
    slots_ref[:, :, 0:128] = jnp.full((slots_ref.shape[0], BLK, 128), EMPTY, BF16)
    for b in range(height // BLK):
        where = dest_ref[b]

        @pl.when(where >= 0)
        def _():
            slots_ref[where] = act_ref[b * BLK : (b + 1) * BLK, :].astype(BF16)

    for copy in copies:
        copy.wait()


def find_senders(flags_ref, table_ref):
    for k in range(table_ref.shape[0]):
        table_ref[k] = 0

    def look(s, count):
        sends = flags_ref[s] > 0

        @pl.when(sends)
        def _():
            table_ref[count] = s

        return count + jnp.where(sends, 1, 0)

    lax.fori_loop(0, flags_ref.shape[0], look, jnp.int32(0))


def scatter_kernel(flags_ref, cot_ref, slots_ref, table_ref):
    find_senders(flags_ref, table_ref)
    for k in range(cot_ref.shape[0] // BLK):
        base = k // 4 * 16
        rows = cot_ref[base : base + 16, :].astype(F32)
        low = k % 4 * BLK
        slots_ref[table_ref[k]] = rows[low : low + BLK, :].astype(BF16)


def load_weight(place_ref, pieces, weight_ref, sems):
    width = pieces[0].shape[1]
    core = place_ref[0]
    copies, row = [], 0
    for i, piece in enumerate(pieces):
        start = core * width if i < len(pieces) // 2 else (1 - core) * width
        row = row % weight_ref.shape[0]
        target = weight_ref.at[pl.ds(row, piece.shape[0]), pl.ds(pl.multiple_of(start, 128), width)]
        copies.append(pltpu.make_async_copy(piece, target, sems.at[i]))
        row += piece.shape[0]
    for copy in copies:
        copy.start()
    return copies


def block_place(place_ref, owner, blocks):
    ny = blocks // (2 * NX)
    oz, ox, oy = owner // (ny * NX), owner // ny % NX, owner % ny
    return ((ox - place_ref[1] + NX) % NX * 2 + oz) * ny + oy


def backward_kernel(
    dest_ref, place_ref, order_ref,
    kernel_ref, gain_ref, inv_ref, slots_ref,
    frames_hbm, unit_hbm, factor_hbm, shift_hbm, p0, p1, p2, p3, p4, q0, q1, q2, q3, q4,
    frame_ref, term_ref,
    frames_ref, unit_ref, factor_ref, shift_ref,
    home_ref, homeb_ref, weight_ref, raw_ref, sorted_ref, grad_ref, moved_ref, sum_ref, sems,
):
    taps = kernel_ref.shape[0]
    height, columns = frames_ref.shape
    blocks = order_ref.shape[0]
    size = columns // blocks
    copies = load_weight(place_ref, (p0, p1, p2, p3, p4, q0, q1, q2, q3, q4), weight_ref, sems)
    saved = [(unit_hbm, unit_ref), (factor_hbm, factor_ref), (shift_hbm, shift_ref), (frames_hbm, frames_ref)]
    late = [pltpu.make_async_copy(a, b, sems.at[len(copies) + i]) for i, (a, b) in enumerate(saved)]
    for copy in late:
        copy.start()
    for b in range(height // BLK):
        where = dest_ref[b]
        rows = slots_ref[jnp.maximum(where, 0)].astype(F32)
        home_ref[b * BLK : (b + 1) * BLK, :] = jnp.where(where >= 0, rows, 0.0)
    homeb_ref[...] = home_ref[...].astype(BF16)
    for copy in copies:
        copy.wait()

    def back(i, carry):
        at = pl.ds(pl.multiple_of(i * 2 * CHUNK, CHUNK), 2 * CHUNK)
        raw_ref[at, :] = lax.dot_general(
            weight_ref[at, :], homeb_ref[...], (((1,), (1,)), ((), ())), preferred_element_type=F32
        )
        return carry

    lax.fori_loop(0, columns // (2 * CHUNK), back, 0)
    for b in range(blocks):
        at = pl.multiple_of(block_place(place_ref, order_ref[b], blocks) * size, 8)
        sorted_ref[b * size : (b + 1) * size, :] = raw_ref[pl.ds(at, size), :]

    def turn(i, carry):
        at = pl.ds(pl.multiple_of(i * CHUNK, CHUNK), CHUNK)
        home_ref[:, at] = sorted_ref[at, :].T.astype(BF16).astype(F32)
        return carry

    lax.fori_loop(0, columns // CHUNK, turn, 0)
    for copy in late:
        copy.wait()
    step = 16
    gain = gain_ref[...]

    def norm(i, total):
        at = pl.ds(pl.multiple_of(i * step, step), step)
        unit = unit_ref[at, :]
        slope = home_ref[at, :] * factor_ref[at, :]
        along = slope * unit
        total = total + along[0:8] + along[8:16]
        slope = slope * gain
        mean_slope = jnp.mean(slope, axis=1, keepdims=True)
        mean_unit = jnp.mean(along * gain, axis=1, keepdims=True)
        grad_ref[at, :] = (inv_ref[at, 0:1] * (slope - mean_slope - unit * mean_unit)).astype(BF16)
        return total

    total = lax.fori_loop(0, height // step, norm, jnp.zeros((8, columns), F32))
    term_ref[taps] = jnp.sum(total, axis=0, keepdims=True)
    part = 64

    def conv(i, carry):
        at = pl.ds(pl.multiple_of(i * CHUNK, CHUNK), CHUNK)
        moved_ref[...] = jnp.dot(shift_ref[...], grad_ref[:, at], preferred_element_type=F32)
        for p in range(height // part):
            rows = slice(p * part, (p + 1) * part)
            frames = frames_ref[rows, at].astype(F32)
            out = jnp.zeros((part, CHUNK), F32)
            for j in range(taps):
                tap = taps - 1 - j
                moved = moved_ref[j * height + p * part : j * height + (p + 1) * part, :]
                out = out + kernel_ref[pl.ds(tap, 1), at] * moved
                add = jnp.sum((frames * moved).reshape(part // 8, 8, CHUNK), axis=0)
                if p == 0:
                    sum_ref[tap] = add
                elif p < height // part - 1:
                    sum_ref[tap] = sum_ref[tap] + add
                else:
                    term_ref[tap, :, at] = jnp.sum(sum_ref[tap] + add, axis=0, keepdims=True)
            frame_ref[rows, at] = out.astype(BF16)
        return carry

    lax.fori_loop(0, columns // CHUNK, conv, 0)


def project_kernel(
    flags_ref, place_ref, order_ref,
    slots_ref, p0, p1, p2, p3, p4, q0, q1, q2, q3, q4,
    out_ref,
    table_ref, rows_ref, turned_ref, weight_ref, sems,
):
    blocks = order_ref.shape[0]
    size = weight_ref.shape[0] // blocks
    copies = load_weight(place_ref, (p0, p1, p2, p3, p4, q0, q1, q2, q3, q4), weight_ref, sems)
    find_senders(flags_ref, table_ref)
    for k in range(rows_ref.shape[0] // BLK):
        rows_ref[k * BLK : (k + 1) * BLK, :] = slots_ref[table_ref[k]].astype(F32)
    turned = rows_ref[...].T
    for b in range(blocks):
        at = pl.multiple_of(block_place(place_ref, order_ref[b], blocks) * size, 8)
        turned_ref[pl.ds(at, size), :] = turned[b * size : (b + 1) * size, :]
    rows = turned_ref[...].T.astype(BF16)
    for copy in copies:
        copy.wait()
    out_ref[...] = jnp.dot(rows, weight_ref[...], preferred_element_type=F32).astype(BF16)


VM = pl.BlockSpec(memory_space=pltpu.VMEM)
SM = pl.BlockSpec(memory_space=pltpu.SMEM)
AN = pl.BlockSpec(memory_space=pl.ANY)
HB = pl.BlockSpec(memory_space=pltpu.HBM)


def call(fn, ins, outs, scratch, mib, name, flops, nbytes, out_specs=None):
    return pl.pallas_call(
        fn,
        in_specs=ins,
        out_specs=out_specs or [VM] * len(outs),
        out_shape=outs,
        scratch_shapes=scratch,
        compiler_params=params(mib),
        cost_estimate=pl.CostEstimate(flops=flops, transcendentals=0, bytes_accessed=nbytes),
        name=name,
    )


def exchange(x, axes):
    return lax.all_to_all(x, axes, split_axis=0, concat_axis=0, tiled=True)


def body(frames, lengths, destination, kernel, norm_gain, master, moment, second, gradient, bucket_order, cotangent):
    height, columns = frames.shape
    taps = kernel.shape[0]
    owners = bucket_order.shape[0]
    half = columns // 2
    core, x = lax.axis_index("c"), lax.axis_index("x")
    dest = destination[0]
    lens = lengths[0]
    place = jnp.stack([core, x]).astype(jnp.int32)
    gain = norm_gain[None, :]

    updated = adam_step(master, moment, second, gradient)
    bucket = lax.dynamic_slice_in_dim(updated, core * half, half, axis=1).astype(BF16)
    near = lax.axis_size(("zl", "y"))
    line = exchange(jnp.broadcast_to(bucket[None], (near, *bucket.shape)), ("zl", "y")).reshape(-1, half)

    slots = jax.ShapeDtypeStruct((owners, BLK, columns), BF16)
    whole = jax.ShapeDtypeStruct((height, columns), F32)
    shifts = jax.ShapeDtypeStruct((taps * height, height), BF16)
    sent, inv, unit, factor, shifts = call(
        forward_kernel,
        [SM, SM, VM, VM, VM],
        [slots, jax.ShapeDtypeStruct((height, 128), F32), whole, whole, shifts],
        [
            pltpu.VMEM(whole.shape, F32),
            pltpu.VMEM(whole.shape, F32),
            pltpu.VMEM(shifts.shape, BF16),
            pltpu.VMEM(whole.shape, F32),
            pltpu.SemaphoreType.DMA((3,)),
        ],
        60,
        "forward",
        8 * taps * height * height * columns,
        16 * height * columns,
        [VM] * 2 + [HB] * 3,
    )(lens, dest, frames, kernel, gain)
    line, sent = lax.optimization_barrier((line, sent))
    act_slots = exchange(sent, DP)

    nx = lax.axis_size("x")
    ahead = [((i + 1) % nx, i) for i in range(nx)]
    behind = [(i, (i + 1) % nx) for i in range(nx)]
    swap = [(0, 1), (1, 0)]
    flags = (act_slots[:, 0, 0] > EMPTY / 2).astype(jnp.int32)
    next_x, last_x = lax.ppermute(line, "x", ahead), lax.ppermute(line, "x", behind)
    line_c = lax.ppermute(line, "c", swap)
    flags, next_x, last_x, line_c = lax.optimization_barrier((flags, next_x, last_x, line_c))
    part = line.shape[0] // 2
    far_low = lax.ppermute(next_x[:part], "x", ahead)
    far_high = lax.ppermute(last_x[part:], "x", behind)
    half_pieces = [line, next_x, far_low, far_high, last_x]
    pieces = half_pieces + [line_c] + [lax.ppermute(piece, "c", swap) for piece in half_pieces[1:]]

    (cot_sent,) = call(
        scatter_kernel, [SM, VM], [slots], [pltpu.SMEM((owners,), jnp.int32)], 60, "scatter", 0, 6 * cotangent.size
    )(flags, cotangent)
    cot_slots = exchange(cot_sent, DP)

    frame_grad, term = call(
        backward_kernel,
        [SM] * 3 + [VM] * 4 + [HB] * 4 + [AN] * 10,
        [
            jax.ShapeDtypeStruct((height, columns), BF16),
            jax.ShapeDtypeStruct((taps + 1, 1, columns), F32),
        ],
        [
            pltpu.VMEM((height, columns), BF16),
            pltpu.VMEM((height, columns), F32),
            pltpu.VMEM((height, columns), F32),
            pltpu.VMEM(shifts.shape, BF16),
            pltpu.VMEM((height, columns), F32),
            pltpu.VMEM((height, columns), BF16),
            pltpu.VMEM((columns, columns), BF16),
            pltpu.VMEM((columns, height), F32),
            pltpu.VMEM((columns, height), F32),
            pltpu.VMEM((height, columns), BF16),
            pltpu.VMEM((taps * height, CHUNK), F32),
            pltpu.VMEM((taps, 8, CHUNK), F32),
            pltpu.SemaphoreType.DMA((14,)),
        ],
        60,
        "backward",
        8 * taps * height * height * columns + 2 * height * columns * columns,
        16 * height * columns + 2 * columns * columns,
    )(dest, place, bucket_order, kernel, gain, inv, cot_slots, frames, unit, factor, shifts, *pieces)

    mine = jnp.sum(exchange(term, NEAR), axis=0, keepdims=True)
    far = lax.axis_size(FAR)
    mine = jnp.sum(exchange(jnp.broadcast_to(mine, (far, 1, columns)), FAR), axis=0, keepdims=True)
    divisor = math.sqrt(lax.axis_size(("zh", "c")) * owners * ROWS)
    sums = exchange(jnp.broadcast_to(mine / divisor, (taps + 1, 1, columns)), NEAR)[:, 0, :]

    (projected,) = call(
        project_kernel,
        [SM] * 3 + [VM] + [AN] * 10,
        [jax.ShapeDtypeStruct(cotangent.shape, BF16)],
        [
            pltpu.SMEM((owners,), jnp.int32),
            pltpu.VMEM(cotangent.shape, F32),
            pltpu.VMEM(cotangent.shape[::-1], F32),
            pltpu.VMEM((columns, columns), BF16),
            pltpu.SemaphoreType.DMA((10,)),
        ],
        60,
        "project",
        2 * cotangent.size * columns,
        4 * cotangent.size + 2 * columns * columns,
    )(flags, place, bucket_order, act_slots, *pieces)
    return projected, frame_grad, sums[:taps], sums[taps], updated


def solution(mesh):
    fine = Mesh(mesh.devices.reshape(4, 2, 2, NX, 8), ("zh", "c", "zl", "x", "y"))
    rep, dp = ("zh", "c"), ("zl", "x", "y")
    every, rows = P(rep + dp, None), P(dp, None)
    return jax.shard_map(
        body,
        mesh=fine,
        in_specs=(every, every, every, P(), P(), rows, rows, rows, rows, P(), every),
        out_specs=(every, every, P(), P(), rows),
        check_vma=False,
    )
```

```python
import math

import jax
import jax.numpy as jnp
from jax import lax
from jax.experimental import pallas as pl
from jax.experimental.pallas import tpu as pltpu
from jax.sharding import Mesh, PartitionSpec as P

ROWS = 128
BLK = 4
CHUNK = 256
EMPTY = -2.0
DP = ("zl", "x", "y")
NEAR = ("c", "zl", "x")
FAR = ("zh", "y")
NX = 4
F32 = jnp.float32
BF16 = jnp.bfloat16


def params(mib):
    return pltpu.CompilerParams(vmem_limit_bytes=mib * 1024 * 1024)


def adam_step(master, moment, second, gradient):
    moment_new = 0.9 * moment + 0.1 * gradient
    second_new = 0.999 * second + 0.001 * jnp.square(gradient)
    return master - 0.01 * (moment_new / (jnp.sqrt(second_new) + 1e-08) + 0.1 * master)


def write_shifts(lengths_ref, shift_ref, taps):
    height = shift_ref.shape[1]
    half = (taps - 1) // 2
    row = lax.broadcasted_iota(jnp.int32, (height, height), 0)
    col = lax.broadcasted_iota(jnp.int32, (height, height), 1)
    bound = jnp.int32(0)
    row_seg = jnp.zeros((height, height), jnp.int32)
    col_seg = jnp.zeros((height, height), jnp.int32)
    for u in range(lengths_ref.shape[0]):
        bound = bound + lengths_ref[u]
        row_seg = row_seg + jnp.where(row >= bound, 1, 0)
        col_seg = col_seg + jnp.where(col >= bound, 1, 0)
    same = (row_seg == col_seg) & (row < bound)
    offset = jnp.where(same, col - row + half, -1)
    for j in range(taps):
        shift_ref[j * height : (j + 1) * height, :] = jnp.where(offset == j, 1.0, 0.0).astype(F32).astype(BF16)


def forward_kernel(
    lengths_ref, dest_ref, frames_ref, kernel_ref, gain_ref,
    slots_ref, inv_ref, unit_hbm, factor_hbm, shift_hbm,
    unit_ref, factor_ref, shift_ref, act_ref, sems,
):
    taps = kernel_ref.shape[0]
    height, columns = frames_ref.shape
    write_shifts(lengths_ref, shift_ref, taps)
    saved = [(shift_ref, shift_hbm), (unit_ref, unit_hbm), (factor_ref, factor_hbm)]
    copies = [pltpu.make_async_copy(a, b, sems.at[i]) for i, (a, b) in enumerate(saved)]
    copies[0].start()

    def conv(i, carry):
        at = pl.ds(pl.multiple_of(i * CHUNK, CHUNK), CHUNK)
        piece = frames_ref[:, at]
        total = jnp.zeros((height, CHUNK), F32)
        for j in range(taps):
            moved = jnp.dot(shift_ref[j * height : (j + 1) * height, :], piece, preferred_element_type=F32)
            total = total + kernel_ref[pl.ds(j, 1), at] * moved
        act_ref[:, at] = total
        return carry

    lax.fori_loop(0, columns // CHUNK, conv, 0)
    step = 16
    gain = gain_ref[...]

    def norm(i, carry):
        at = pl.ds(pl.multiple_of(i * step, step), step)
        mixed = act_ref[at, :]
        center = jnp.mean(mixed, axis=1, keepdims=True)
        off = mixed - center
        inv = lax.rsqrt(jnp.mean(off * off, axis=1, keepdims=True) + 1e-05)
        unit = off * inv
        scaled = unit * gain
        sig = jax.nn.sigmoid(scaled)
        act = scaled * sig
        act_ref[at, :] = act
        unit_ref[at, :] = unit
        factor_ref[at, :] = sig + act * (1.0 - sig)
        inv_ref[at, :] = jnp.broadcast_to(inv, (step, inv_ref.shape[1]))
        return carry

    lax.fori_loop(0, height // step, norm, 0)
    copies[1].start()
    copies[2].start()
    slots_ref[:, :, 0:128] = jnp.full((slots_ref.shape[0], BLK, 128), EMPTY, BF16)
    for b in range(height // BLK):
        where = dest_ref[b]

        @pl.when(where >= 0)
        def _():
            slots_ref[where] = act_ref[b * BLK : (b + 1) * BLK, :].astype(BF16)

    for copy in copies:
        copy.wait()


def find_senders(flags_ref, table_ref):
    for k in range(table_ref.shape[0]):
        table_ref[k] = 0

    def look(s, count):
        sends = flags_ref[s] > 0

        @pl.when(sends)
        def _():
            table_ref[count] = s

        return count + jnp.where(sends, 1, 0)

    lax.fori_loop(0, flags_ref.shape[0], look, jnp.int32(0))


def scatter_kernel(flags_ref, cot_ref, slots_ref, table_ref):
    find_senders(flags_ref, table_ref)
    for k in range(cot_ref.shape[0] // BLK):
        base = k // 4 * 16
        rows = cot_ref[base : base + 16, :].astype(F32)
        low = k % 4 * BLK
        slots_ref[table_ref[k]] = rows[low : low + BLK, :].astype(BF16)


def load_weight(place_ref, pieces, weight_ref, sems):
    count = len(pieces) // 2
    width = pieces[0].shape[1]
    core = place_ref[0]
    groups, row = [], 0
    for i in range(count):
        rows = pieces[i].shape[0]
        copies = []
        for h in range(2):
            start = core * width if h == 0 else (1 - core) * width
            target = weight_ref.at[pl.ds(row, rows), pl.ds(pl.multiple_of(start, 128), width)]
            copies.append(pltpu.make_async_copy(pieces[h * count + i], target, sems.at[2 * i + h]))
            copies[h].start()
        groups.append((row, rows, copies))
        row += rows
    return groups


def block_place(place_ref, owner, blocks):
    ny = blocks // (2 * NX)
    oz, ox, oy = owner // (ny * NX), owner // ny % NX, owner % ny
    return ((ox - place_ref[1] + NX) % NX * 2 + oz) * ny + oy


def backward_kernel(
    dest_ref, place_ref, order_ref,
    kernel_ref, gain_ref, inv_ref, slots_ref,
    frames_hbm, unit_hbm, factor_hbm, shift_hbm, p0, p1, p2, p3, p4, q0, q1, q2, q3, q4,
    frame_ref, term_ref,
    frames_ref, unit_ref, factor_ref, shift_ref,
    home_ref, homeb_ref, weight_ref, raw_ref, sorted_ref, grad_ref, moved_ref, sum_ref, sems,
):
    taps = kernel_ref.shape[0]
    height, columns = frames_ref.shape
    blocks = order_ref.shape[0]
    size = columns // blocks
    groups = load_weight(place_ref, (p0, p1, p2, p3, p4, q0, q1, q2, q3, q4), weight_ref, sems)
    saved = [(unit_hbm, unit_ref), (factor_hbm, factor_ref), (shift_hbm, shift_ref), (frames_hbm, frames_ref)]
    late = [pltpu.make_async_copy(a, b, sems.at[2 * len(groups) + i]) for i, (a, b) in enumerate(saved)]
    for copy in late:
        copy.start()
    for b in range(height // BLK):
        where = dest_ref[b]
        rows = slots_ref[jnp.maximum(where, 0)].astype(F32)
        home_ref[b * BLK : (b + 1) * BLK, :] = jnp.where(where >= 0, rows, 0.0)
    homeb_ref[...] = home_ref[...].astype(BF16)
    for row, rows, copies in groups:
        for copy in copies:
            copy.wait()
        raw_ref[row : row + rows, :] = lax.dot_general(
            weight_ref[row : row + rows, :], homeb_ref[...], (((1,), (1,)), ((), ())), preferred_element_type=F32
        )
    for b in range(blocks):
        at = pl.multiple_of(block_place(place_ref, order_ref[b], blocks) * size, 8)
        sorted_ref[b * size : (b + 1) * size, :] = raw_ref[pl.ds(at, size), :]

    def turn(i, carry):
        at = pl.ds(pl.multiple_of(i * CHUNK, CHUNK), CHUNK)
        home_ref[:, at] = sorted_ref[at, :].astype(BF16).T.astype(F32)
        return carry

    lax.fori_loop(0, columns // CHUNK, turn, 0)
    for copy in late:
        copy.wait()
    step = 16
    gain = gain_ref[...]

    def norm(i, total):
        at = pl.ds(pl.multiple_of(i * step, step), step)
        unit = unit_ref[at, :]
        slope = home_ref[at, :] * factor_ref[at, :]
        along = slope * unit
        total = total + along[0:8] + along[8:16]
        slope = slope * gain
        mean_slope = jnp.mean(slope, axis=1, keepdims=True)
        mean_unit = jnp.mean(along * gain, axis=1, keepdims=True)
        grad_ref[at, :] = (inv_ref[at, 0:1] * (slope - mean_slope - unit * mean_unit)).astype(BF16)
        return total

    total = lax.fori_loop(0, height // step, norm, jnp.zeros((8, columns), F32))
    term_ref[taps] = jnp.sum(total, axis=0, keepdims=True)
    part = 64

    def conv(i, carry):
        at = pl.ds(pl.multiple_of(i * CHUNK, CHUNK), CHUNK)
        moved_ref[...] = jnp.dot(shift_ref[...], grad_ref[:, at], preferred_element_type=F32)
        for p in range(height // part):
            rows = slice(p * part, (p + 1) * part)
            frames = frames_ref[rows, at].astype(F32)
            out = jnp.zeros((part, CHUNK), F32)
            for j in range(taps):
                tap = taps - 1 - j
                moved = moved_ref[j * height + p * part : j * height + (p + 1) * part, :]
                out = out + kernel_ref[pl.ds(tap, 1), at] * moved
                add = jnp.sum((frames * moved).reshape(part // 8, 8, CHUNK), axis=0)
                if p == 0:
                    sum_ref[tap] = add
                elif p < height // part - 1:
                    sum_ref[tap] = sum_ref[tap] + add
                else:
                    term_ref[tap, :, at] = jnp.sum(sum_ref[tap] + add, axis=0, keepdims=True)
            frame_ref[rows, at] = out.astype(BF16)
        return carry

    lax.fori_loop(0, columns // CHUNK, conv, 0)


def project_kernel(
    flags_ref, place_ref, order_ref,
    slots_ref, p0, p1, p2, p3, p4, q0, q1, q2, q3, q4,
    out_ref,
    table_ref, rows_ref, turned_ref, weight_ref, sems,
):
    blocks = order_ref.shape[0]
    size = weight_ref.shape[0] // blocks
    groups = load_weight(place_ref, (p0, p1, p2, p3, p4, q0, q1, q2, q3, q4), weight_ref, sems)
    find_senders(flags_ref, table_ref)
    for k in range(rows_ref.shape[0] // BLK):
        rows_ref[k * BLK : (k + 1) * BLK, :] = slots_ref[table_ref[k]].astype(F32)
    turned = rows_ref[...].T
    for b in range(blocks):
        at = pl.multiple_of(block_place(place_ref, order_ref[b], blocks) * size, 8)
        turned_ref[pl.ds(at, size), :] = turned[b * size : (b + 1) * size, :]
    rows = turned_ref[...].T.astype(BF16)
    for _, _, copies in groups:
        for copy in copies:
            copy.wait()
    out_ref[...] = jnp.dot(rows, weight_ref[...], preferred_element_type=F32).astype(BF16)


VM = pl.BlockSpec(memory_space=pltpu.VMEM)
SM = pl.BlockSpec(memory_space=pltpu.SMEM)
AN = pl.BlockSpec(memory_space=pl.ANY)
HB = pl.BlockSpec(memory_space=pltpu.HBM)


def call(fn, ins, outs, scratch, mib, name, flops, nbytes, out_specs=None):
    return pl.pallas_call(
        fn,
        in_specs=ins,
        out_specs=out_specs or [VM] * len(outs),
        out_shape=outs,
        scratch_shapes=scratch,
        compiler_params=params(mib),
        cost_estimate=pl.CostEstimate(flops=flops, transcendentals=0, bytes_accessed=nbytes),
        name=name,
    )


def exchange(x, axes):
    return lax.all_to_all(x, axes, split_axis=0, concat_axis=0, tiled=True)


def body(frames, lengths, destination, kernel, norm_gain, master, moment, second, gradient, bucket_order, cotangent):
    height, columns = frames.shape
    taps = kernel.shape[0]
    owners = bucket_order.shape[0]
    half = columns // 2
    core, x = lax.axis_index("c"), lax.axis_index("x")
    dest = destination[0]
    lens = lengths[0]
    place = jnp.stack([core, x]).astype(jnp.int32)
    gain = norm_gain[None, :]

    updated = adam_step(master, moment, second, gradient)
    bucket = lax.dynamic_slice_in_dim(updated, core * half, half, axis=1).astype(BF16)
    near = lax.axis_size(("zl", "y"))
    line = exchange(jnp.broadcast_to(bucket[None], (near, *bucket.shape)), ("zl", "y")).reshape(-1, half)

    slots = jax.ShapeDtypeStruct((owners, BLK, columns), BF16)
    whole = jax.ShapeDtypeStruct((height, columns), F32)
    shifts = jax.ShapeDtypeStruct((taps * height, height), BF16)
    sent, inv, unit, factor, shifts = call(
        forward_kernel,
        [SM, SM, VM, VM, VM],
        [slots, jax.ShapeDtypeStruct((height, 128), F32), whole, whole, shifts],
        [
            pltpu.VMEM(whole.shape, F32),
            pltpu.VMEM(whole.shape, F32),
            pltpu.VMEM(shifts.shape, BF16),
            pltpu.VMEM(whole.shape, F32),
            pltpu.SemaphoreType.DMA((3,)),
        ],
        60,
        "forward",
        8 * taps * height * height * columns,
        16 * height * columns,
        [VM] * 2 + [HB] * 3,
    )(lens, dest, frames, kernel, gain)
    line, sent = lax.optimization_barrier((line, sent))
    act_slots = exchange(sent, DP)

    nx = lax.axis_size("x")
    ahead = [((i + 1) % nx, i) for i in range(nx)]
    behind = [(i, (i + 1) % nx) for i in range(nx)]
    swap = [(0, 1), (1, 0)]
    flags = (act_slots[:, 0, 0] > EMPTY / 2).astype(jnp.int32)
    next_x, last_x = lax.ppermute(line, "x", ahead), lax.ppermute(line, "x", behind)
    line_c = lax.ppermute(line, "c", swap)
    (cot_sent,) = call(
        scatter_kernel, [SM, VM], [slots], [pltpu.SMEM((owners,), jnp.int32)], 60, "scatter", 0, 6 * cotangent.size
    )(flags, cotangent)
    cot_sent, next_x, last_x, line_c = lax.optimization_barrier((cot_sent, next_x, last_x, line_c))
    cot_slots = exchange(cot_sent, DP)
    part = line.shape[0] // 2
    far_low = lax.ppermute(next_x[:part], "x", ahead)
    far_high = lax.ppermute(last_x[part:], "x", behind)
    half_pieces = [line, next_x, far_low, far_high, last_x]
    pieces = half_pieces + [line_c] + [lax.ppermute(piece, "c", swap) for piece in half_pieces[1:]]

    frame_grad, term = call(
        backward_kernel,
        [SM] * 3 + [VM] * 4 + [HB] * 4 + [AN] * 10,
        [
            jax.ShapeDtypeStruct((height, columns), BF16),
            jax.ShapeDtypeStruct((taps + 1, 1, columns), F32),
        ],
        [
            pltpu.VMEM((height, columns), BF16),
            pltpu.VMEM((height, columns), F32),
            pltpu.VMEM((height, columns), F32),
            pltpu.VMEM(shifts.shape, BF16),
            pltpu.VMEM((height, columns), F32),
            pltpu.VMEM((height, columns), BF16),
            pltpu.VMEM((columns, columns), BF16),
            pltpu.VMEM((columns, height), F32),
            pltpu.VMEM((columns, height), F32),
            pltpu.VMEM((height, columns), BF16),
            pltpu.VMEM((taps * height, CHUNK), F32),
            pltpu.VMEM((taps, 8, CHUNK), F32),
            pltpu.SemaphoreType.DMA((14,)),
        ],
        60,
        "backward",
        8 * taps * height * height * columns + 2 * height * columns * columns,
        16 * height * columns + 2 * columns * columns,
    )(dest, place, bucket_order, kernel, gain, inv, cot_slots, frames, unit, factor, shifts, *pieces)

    mine = jnp.sum(exchange(term, NEAR), axis=0, keepdims=True)
    far = lax.axis_size(FAR)
    mine = jnp.sum(exchange(jnp.broadcast_to(mine, (far, 1, columns)), FAR), axis=0, keepdims=True)
    divisor = math.sqrt(lax.axis_size(("zh", "c")) * owners * ROWS)
    sums = exchange(jnp.broadcast_to(mine / divisor, (taps + 1, 1, columns)), NEAR)[:, 0, :]

    (projected,) = call(
        project_kernel,
        [SM] * 3 + [VM] + [AN] * 10,
        [jax.ShapeDtypeStruct(cotangent.shape, BF16)],
        [
            pltpu.SMEM((owners,), jnp.int32),
            pltpu.VMEM(cotangent.shape, F32),
            pltpu.VMEM(cotangent.shape[::-1], F32),
            pltpu.VMEM((columns, columns), BF16),
            pltpu.SemaphoreType.DMA((10,)),
        ],
        60,
        "project",
        2 * cotangent.size * columns,
        4 * cotangent.size + 2 * columns * columns,
    )(flags, place, bucket_order, act_slots, *pieces)
    return projected, frame_grad, sums[:taps], sums[taps], updated


def solution(mesh):
    fine = Mesh(mesh.devices.reshape(4, 2, 2, NX, 8), ("zh", "c", "zl", "x", "y"))
    rep, dp = ("zh", "c"), ("zl", "x", "y")
    every, rows = P(rep + dp, None), P(dp, None)
    return jax.shard_map(
        body,
        mesh=fine,
        in_specs=(every, every, every, P(), P(), rows, rows, rows, rows, P(), every),
        out_specs=(every, every, P(), P(), rows),
        check_vma=False,
    )
```

```python
import math

import jax
import jax.numpy as jnp
from jax import lax
from jax.experimental import pallas as pl
from jax.experimental.pallas import tpu as pltpu
from jax.sharding import Mesh, PartitionSpec as P

ROWS = 128
BLK = 4
CHUNK = 256
EMPTY = -2.0
DP = ("zl", "x", "y")
NEAR = ("c", "zl", "x")
FAR = ("zh", "y")
NX = 4
F32 = jnp.float32
BF16 = jnp.bfloat16


def params(mib):
    return pltpu.CompilerParams(vmem_limit_bytes=mib * 1024 * 1024)


def adam_step(master, moment, second, gradient):
    moment_new = 0.9 * moment + 0.1 * gradient
    second_new = 0.999 * second + 0.001 * jnp.square(gradient)
    return master - 0.01 * (moment_new / (jnp.sqrt(second_new) + 1e-08) + 0.1 * master)


def write_shifts(lengths_ref, shift_ref, taps):
    height = shift_ref.shape[1]
    half = (taps - 1) // 2
    row = lax.broadcasted_iota(jnp.int32, (height, height), 0)
    col = lax.broadcasted_iota(jnp.int32, (height, height), 1)
    bound = jnp.int32(0)
    row_seg = jnp.zeros((height, height), jnp.int32)
    col_seg = jnp.zeros((height, height), jnp.int32)
    for u in range(lengths_ref.shape[0]):
        bound = bound + lengths_ref[u]
        row_seg = row_seg + jnp.where(row >= bound, 1, 0)
        col_seg = col_seg + jnp.where(col >= bound, 1, 0)
    same = (row_seg == col_seg) & (row < bound)
    offset = jnp.where(same, col - row + half, -1)
    for j in range(taps):
        shift_ref[j * height : (j + 1) * height, :] = jnp.where(offset == j, 1.0, 0.0).astype(F32).astype(BF16)


def forward_kernel(
    lengths_ref, dest_ref, frames_ref, kernel_ref, gain_ref,
    slots_ref, inv_ref, unit_hbm, factor_hbm, shift_hbm,
    unit_ref, factor_ref, shift_ref, act_ref, sems,
):
    taps = kernel_ref.shape[0]
    height, columns = frames_ref.shape
    write_shifts(lengths_ref, shift_ref, taps)
    saved = [(shift_ref, shift_hbm), (unit_ref, unit_hbm), (factor_ref, factor_hbm)]
    copies = [pltpu.make_async_copy(a, b, sems.at[i]) for i, (a, b) in enumerate(saved)]
    copies[0].start()

    def conv(i, carry):
        at = pl.ds(pl.multiple_of(i * CHUNK, CHUNK), CHUNK)
        piece = frames_ref[:, at]
        total = jnp.zeros((height, CHUNK), F32)
        for j in range(taps):
            moved = jnp.dot(shift_ref[j * height : (j + 1) * height, :], piece, preferred_element_type=F32)
            total = total + kernel_ref[pl.ds(j, 1), at] * moved
        act_ref[:, at] = total
        return carry

    lax.fori_loop(0, columns // CHUNK, conv, 0)
    step = 16
    gain = gain_ref[...]

    def norm(i, carry):
        at = pl.ds(pl.multiple_of(i * step, step), step)
        mixed = act_ref[at, :]
        center = jnp.mean(mixed, axis=1, keepdims=True)
        off = mixed - center
        inv = lax.rsqrt(jnp.mean(off * off, axis=1, keepdims=True) + 1e-05)
        unit = off * inv
        scaled = unit * gain
        sig = jax.nn.sigmoid(scaled)
        act = scaled * sig
        act_ref[at, :] = act
        unit_ref[at, :] = unit
        factor_ref[at, :] = sig + act * (1.0 - sig)
        inv_ref[at, :] = jnp.broadcast_to(inv, (step, inv_ref.shape[1]))
        return carry

    lax.fori_loop(0, height // step, norm, 0)
    copies[1].start()
    copies[2].start()
    slots_ref[:, :, 0:128] = jnp.full((slots_ref.shape[0], BLK, 128), EMPTY, BF16)
    for b in range(height // BLK):
        where = dest_ref[b]

        @pl.when(where >= 0)
        def _():
            slots_ref[where] = act_ref[b * BLK : (b + 1) * BLK, :].astype(BF16)

    for copy in copies:
        copy.wait()


def find_senders(flags_ref, table_ref):
    for k in range(table_ref.shape[0]):
        table_ref[k] = 0

    def look(s, count):
        sends = flags_ref[s] > 0

        @pl.when(sends)
        def _():
            table_ref[count] = s

        return count + jnp.where(sends, 1, 0)

    lax.fori_loop(0, flags_ref.shape[0], look, jnp.int32(0))


def scatter_kernel(flags_ref, cot_ref, slots_ref, table_ref):
    find_senders(flags_ref, table_ref)
    for k in range(cot_ref.shape[0] // BLK):
        base = k // 4 * 16
        rows = cot_ref[base : base + 16, :].astype(F32)
        low = k % 4 * BLK
        slots_ref[table_ref[k]] = rows[low : low + BLK, :].astype(BF16)


def load_weight(place_ref, pieces, weight_ref, sems):
    count = len(pieces) // 2
    width = pieces[0].shape[1]
    core = place_ref[0]
    groups, row = [], 0
    for i in range(count):
        rows = pieces[i].shape[0]
        copies = []
        for h in range(2):
            start = core * width if h == 0 else (1 - core) * width
            target = weight_ref.at[pl.ds(row, rows), pl.ds(pl.multiple_of(start, 128), width)]
            copies.append(pltpu.make_async_copy(pieces[h * count + i], target, sems.at[2 * i + h]))
            copies[h].start()
        groups.append((row, rows, copies))
        row += rows
    return groups


def block_place(place_ref, owner, blocks):
    ny = blocks // (2 * NX)
    oz, ox, oy = owner // (ny * NX), owner // ny % NX, owner % ny
    return ((ox - place_ref[1] + NX) % NX * 2 + oz) * ny + oy


def backward_kernel(
    dest_ref, place_ref, order_ref,
    kernel_ref, gain_ref, inv_ref, slots_ref,
    frames_hbm, unit_hbm, factor_hbm, shift_hbm, p0, p1, p2, p3, p4, q0, q1, q2, q3, q4,
    frame_ref, term_ref,
    frames_ref, unit_ref, factor_ref, shift_ref,
    home_ref, homeb_ref, weight_ref, raw_ref, sorted_ref, grad_ref, moved_ref, sum_ref, sems,
):
    taps = kernel_ref.shape[0]
    height, columns = frames_ref.shape
    blocks = order_ref.shape[0]
    size = columns // blocks
    groups = load_weight(place_ref, (p0, p1, p2, p3, p4, q0, q1, q2, q3, q4), weight_ref, sems)
    saved = [(unit_hbm, unit_ref), (factor_hbm, factor_ref), (shift_hbm, shift_ref), (frames_hbm, frames_ref)]
    late = [pltpu.make_async_copy(a, b, sems.at[2 * len(groups) + i]) for i, (a, b) in enumerate(saved)]
    for copy in late:
        copy.start()
    for b in range(height // BLK):
        where = dest_ref[b]
        rows = slots_ref[jnp.maximum(where, 0)].astype(F32)
        home_ref[b * BLK : (b + 1) * BLK, :] = jnp.where(where >= 0, rows, 0.0)
    homeb_ref[...] = home_ref[...].astype(BF16)
    for row, rows, copies in groups:
        for copy in copies:
            copy.wait()
        raw_ref[row : row + rows, :] = lax.dot_general(
            weight_ref[row : row + rows, :], homeb_ref[...], (((1,), (1,)), ((), ())), preferred_element_type=F32
        )
    for b in range(blocks):
        at = pl.multiple_of(block_place(place_ref, order_ref[b], blocks) * size, 8)
        sorted_ref[b * size : (b + 1) * size, :] = raw_ref[pl.ds(at, size), :]

    def turn(i, carry):
        at = pl.ds(pl.multiple_of(i * CHUNK, CHUNK), CHUNK)
        home_ref[:, at] = sorted_ref[at, :].astype(BF16).T.astype(F32)
        return carry

    lax.fori_loop(0, columns // CHUNK, turn, 0)
    for copy in late:
        copy.wait()
    step = 16
    gain = gain_ref[...]

    def norm(i, total):
        at = pl.ds(pl.multiple_of(i * step, step), step)
        unit = unit_ref[at, :]
        slope = home_ref[at, :] * factor_ref[at, :]
        along = slope * unit
        total = total + along[0:8] + along[8:16]
        slope = slope * gain
        mean_slope = jnp.mean(slope, axis=1, keepdims=True)
        mean_unit = jnp.mean(along * gain, axis=1, keepdims=True)
        grad_ref[at, :] = (inv_ref[at, 0:1] * (slope - mean_slope - unit * mean_unit)).astype(BF16)
        return total

    total = lax.fori_loop(0, height // step, norm, jnp.zeros((8, columns), F32))
    term_ref[taps] = jnp.sum(total, axis=0, keepdims=True)
    part = 64

    def conv(i, carry):
        at = pl.ds(pl.multiple_of(i * CHUNK, CHUNK), CHUNK)
        moved_ref[...] = jnp.dot(shift_ref[...], grad_ref[:, at], preferred_element_type=F32)
        for p in range(height // part):
            rows = slice(p * part, (p + 1) * part)
            frames = frames_ref[rows, at].astype(F32)
            out = jnp.zeros((part, CHUNK), F32)
            for j in range(taps):
                tap = taps - 1 - j
                moved = moved_ref[j * height + p * part : j * height + (p + 1) * part, :]
                out = out + kernel_ref[pl.ds(tap, 1), at] * moved
                add = jnp.sum((frames * moved).reshape(part // 8, 8, CHUNK), axis=0)
                if p == 0:
                    sum_ref[tap] = add
                elif p < height // part - 1:
                    sum_ref[tap] = sum_ref[tap] + add
                else:
                    term_ref[tap, :, at] = jnp.sum(sum_ref[tap] + add, axis=0, keepdims=True)
            frame_ref[rows, at] = out.astype(BF16)
        return carry

    lax.fori_loop(0, columns // CHUNK, conv, 0)


def project_kernel(
    flags_ref, place_ref, order_ref,
    slots_ref, p0, p1, p2, p3, p4, q0, q1, q2, q3, q4,
    out_ref,
    table_ref, rows_ref, turned_ref, weight_ref, sems,
):
    blocks = order_ref.shape[0]
    size = weight_ref.shape[0] // blocks
    groups = load_weight(place_ref, (p0, p1, p2, p3, p4, q0, q1, q2, q3, q4), weight_ref, sems)
    find_senders(flags_ref, table_ref)
    for k in range(rows_ref.shape[0] // BLK):
        rows_ref[k * BLK : (k + 1) * BLK, :] = slots_ref[table_ref[k]].astype(F32)
    turned = rows_ref[...].T
    for b in range(blocks):
        at = pl.multiple_of(block_place(place_ref, order_ref[b], blocks) * size, 8)
        turned_ref[pl.ds(at, size), :] = turned[b * size : (b + 1) * size, :]
    rows = turned_ref[...].T.astype(BF16)
    for _, _, copies in groups:
        for copy in copies:
            copy.wait()
    out_ref[...] = jnp.dot(rows, weight_ref[...], preferred_element_type=F32).astype(BF16)


VM = pl.BlockSpec(memory_space=pltpu.VMEM)
SM = pl.BlockSpec(memory_space=pltpu.SMEM)
AN = pl.BlockSpec(memory_space=pl.ANY)
HB = pl.BlockSpec(memory_space=pltpu.HBM)


def call(fn, ins, outs, scratch, mib, name, flops, nbytes, out_specs=None):
    return pl.pallas_call(
        fn,
        in_specs=ins,
        out_specs=out_specs or [VM] * len(outs),
        out_shape=outs,
        scratch_shapes=scratch,
        compiler_params=params(mib),
        cost_estimate=pl.CostEstimate(flops=flops, transcendentals=0, bytes_accessed=nbytes),
        name=name,
    )


def exchange(x, axes):
    return lax.all_to_all(x, axes, split_axis=0, concat_axis=0, tiled=True)


def body(frames, lengths, destination, kernel, norm_gain, master, moment, second, gradient, bucket_order, cotangent):
    height, columns = frames.shape
    taps = kernel.shape[0]
    owners = bucket_order.shape[0]
    half = columns // 2
    core, x = lax.axis_index("c"), lax.axis_index("x")
    dest = destination[0]
    lens = lengths[0]
    place = jnp.stack([core, x]).astype(jnp.int32)
    gain = norm_gain[None, :]

    updated = adam_step(master, moment, second, gradient)
    bucket = lax.dynamic_slice_in_dim(updated, core * half, half, axis=1).astype(BF16)
    near = lax.axis_size(("zl", "y"))
    line = exchange(jnp.broadcast_to(bucket[None], (near, *bucket.shape)), ("zl", "y")).reshape(-1, half)

    slots = jax.ShapeDtypeStruct((owners, BLK, columns), BF16)
    whole = jax.ShapeDtypeStruct((height, columns), F32)
    shifts = jax.ShapeDtypeStruct((taps * height, height), BF16)
    sent, inv, unit, factor, shifts = call(
        forward_kernel,
        [SM, SM, VM, VM, VM],
        [slots, jax.ShapeDtypeStruct((height, 128), F32), whole, whole, shifts],
        [
            pltpu.VMEM(whole.shape, F32),
            pltpu.VMEM(whole.shape, F32),
            pltpu.VMEM(shifts.shape, BF16),
            pltpu.VMEM(whole.shape, F32),
            pltpu.SemaphoreType.DMA((3,)),
        ],
        60,
        "forward",
        8 * taps * height * height * columns,
        16 * height * columns,
        [VM] * 2 + [HB] * 3,
    )(lens, dest, frames, kernel, gain)
    line, sent = lax.optimization_barrier((line, sent))
    act_slots = exchange(sent, DP)

    nx = lax.axis_size("x")
    ahead = [((i + 1) % nx, i) for i in range(nx)]
    behind = [(i, (i + 1) % nx) for i in range(nx)]
    swap = [(0, 1), (1, 0)]
    flags = (act_slots[:, 0, 0] > EMPTY / 2).astype(jnp.int32)
    next_x, last_x = lax.ppermute(line, "x", ahead), lax.ppermute(line, "x", behind)
    line_c = lax.ppermute(line, "c", swap)
    (cot_sent,) = call(
        scatter_kernel, [SM, VM], [slots], [pltpu.SMEM((owners,), jnp.int32)], 60, "scatter", 0, 6 * cotangent.size
    )(flags, cotangent)
    part = line.shape[0] // 2
    far_low = lax.ppermute(next_x[:part], "x", ahead)
    far_high = lax.ppermute(last_x[part:], "x", behind)
    cot_sent, next_x, last_x, line_c, far_low, far_high = lax.optimization_barrier(
        (cot_sent, next_x, last_x, line_c, far_low, far_high)
    )
    cot_slots = exchange(cot_sent, DP)
    half_pieces = [line, next_x, far_low, far_high, last_x]
    pieces = half_pieces + [line_c] + [lax.ppermute(piece, "c", swap) for piece in half_pieces[1:]]

    frame_grad, term = call(
        backward_kernel,
        [SM] * 3 + [VM] * 4 + [HB] * 4 + [AN] * 10,
        [
            jax.ShapeDtypeStruct((height, columns), BF16),
            jax.ShapeDtypeStruct((taps + 1, 1, columns), F32),
        ],
        [
            pltpu.VMEM((height, columns), BF16),
            pltpu.VMEM((height, columns), F32),
            pltpu.VMEM((height, columns), F32),
            pltpu.VMEM(shifts.shape, BF16),
            pltpu.VMEM((height, columns), F32),
            pltpu.VMEM((height, columns), BF16),
            pltpu.VMEM((columns, columns), BF16),
            pltpu.VMEM((columns, height), F32),
            pltpu.VMEM((columns, height), F32),
            pltpu.VMEM((height, columns), BF16),
            pltpu.VMEM((taps * height, CHUNK), F32),
            pltpu.VMEM((taps, 8, CHUNK), F32),
            pltpu.SemaphoreType.DMA((14,)),
        ],
        60,
        "backward",
        8 * taps * height * height * columns + 2 * height * columns * columns,
        16 * height * columns + 2 * columns * columns,
    )(dest, place, bucket_order, kernel, gain, inv, cot_slots, frames, unit, factor, shifts, *pieces)

    mine = jnp.sum(exchange(term, NEAR), axis=0, keepdims=True)
    far = lax.axis_size(FAR)
    mine = jnp.sum(exchange(jnp.broadcast_to(mine, (far, 1, columns)), FAR), axis=0, keepdims=True)
    divisor = math.sqrt(lax.axis_size(("zh", "c")) * owners * ROWS)
    sums = exchange(jnp.broadcast_to(mine / divisor, (taps + 1, 1, columns)), NEAR)[:, 0, :]

    (projected,) = call(
        project_kernel,
        [SM] * 3 + [VM] + [AN] * 10,
        [jax.ShapeDtypeStruct(cotangent.shape, BF16)],
        [
            pltpu.SMEM((owners,), jnp.int32),
            pltpu.VMEM(cotangent.shape, F32),
            pltpu.VMEM(cotangent.shape[::-1], F32),
            pltpu.VMEM((columns, columns), BF16),
            pltpu.SemaphoreType.DMA((10,)),
        ],
        60,
        "project",
        2 * cotangent.size * columns,
        4 * cotangent.size + 2 * columns * columns,
    )(flags, place, bucket_order, act_slots, *pieces)
    return projected, frame_grad, sums[:taps], sums[taps], updated


def solution(mesh):
    fine = Mesh(mesh.devices.reshape(4, 2, 2, NX, 8), ("zh", "c", "zl", "x", "y"))
    rep, dp = ("zh", "c"), ("zl", "x", "y")
    every, rows = P(rep + dp, None), P(dp, None)
    return jax.shard_map(
        body,
        mesh=fine,
        in_specs=(every, every, every, P(), P(), rows, rows, rows, rows, P(), every),
        out_specs=(every, every, P(), P(), rows),
        check_vma=False,
    )
```

```python
import math

import jax
import jax.numpy as jnp
from jax import lax
from jax.experimental import pallas as pl
from jax.experimental.pallas import tpu as pltpu
from jax.sharding import Mesh, PartitionSpec as P

ROWS = 128
BLK = 4
CHUNK = 256
EMPTY = -2.0
DP = ("zl", "x", "y")
NEAR = ("c", "zl", "x")
FAR = ("zh", "y")
NX = 4
F32 = jnp.float32
BF16 = jnp.bfloat16


def params(mib):
    return pltpu.CompilerParams(vmem_limit_bytes=mib * 1024 * 1024)


def adam_step(master, moment, second, gradient):
    moment_new = 0.9 * moment + 0.1 * gradient
    second_new = 0.999 * second + 0.001 * jnp.square(gradient)
    return master - 0.01 * (moment_new / (jnp.sqrt(second_new) + 1e-08) + 0.1 * master)


def write_shifts(lengths_ref, shift_ref, taps):
    height = shift_ref.shape[1]
    half = (taps - 1) // 2
    row = lax.broadcasted_iota(jnp.int32, (height, height), 0)
    col = lax.broadcasted_iota(jnp.int32, (height, height), 1)
    bound = jnp.int32(0)
    row_seg = jnp.zeros((height, height), jnp.int32)
    col_seg = jnp.zeros((height, height), jnp.int32)
    for u in range(lengths_ref.shape[0]):
        bound = bound + lengths_ref[u]
        row_seg = row_seg + jnp.where(row >= bound, 1, 0)
        col_seg = col_seg + jnp.where(col >= bound, 1, 0)
    same = (row_seg == col_seg) & (row < bound)
    offset = jnp.where(same, col - row + half, -1)
    for j in range(taps):
        shift_ref[j * height : (j + 1) * height, :] = jnp.where(offset == j, 1.0, 0.0).astype(F32).astype(BF16)


def forward_kernel(
    lengths_ref, dest_ref, frames_ref, kernel_ref, gain_ref,
    slots_ref, inv_ref, unit_hbm, factor_hbm, shift_hbm,
    unit_ref, factor_ref, shift_ref, act_ref, sems,
):
    taps = kernel_ref.shape[0]
    height, columns = frames_ref.shape
    write_shifts(lengths_ref, shift_ref, taps)
    saved = [(shift_ref, shift_hbm), (unit_ref, unit_hbm), (factor_ref, factor_hbm)]
    copies = [pltpu.make_async_copy(a, b, sems.at[i]) for i, (a, b) in enumerate(saved)]
    copies[0].start()

    def conv(i, carry):
        at = pl.ds(pl.multiple_of(i * CHUNK, CHUNK), CHUNK)
        piece = frames_ref[:, at]
        total = jnp.zeros((height, CHUNK), F32)
        for j in range(taps):
            moved = jnp.dot(shift_ref[j * height : (j + 1) * height, :], piece, preferred_element_type=F32)
            total = total + kernel_ref[pl.ds(j, 1), at] * moved
        act_ref[:, at] = total
        return carry

    lax.fori_loop(0, columns // CHUNK, conv, 0)
    step = 16
    gain = gain_ref[...]

    def norm(i, carry):
        at = pl.ds(pl.multiple_of(i * step, step), step)
        mixed = act_ref[at, :]
        center = jnp.mean(mixed, axis=1, keepdims=True)
        off = mixed - center
        inv = lax.rsqrt(jnp.mean(off * off, axis=1, keepdims=True) + 1e-05)
        unit = off * inv
        scaled = unit * gain
        sig = jax.nn.sigmoid(scaled)
        act = scaled * sig
        act_ref[at, :] = act
        unit_ref[at, :] = unit
        factor_ref[at, :] = sig + act * (1.0 - sig)
        inv_ref[at, :] = jnp.broadcast_to(inv, (step, inv_ref.shape[1]))
        return carry

    lax.fori_loop(0, height // step, norm, 0)
    copies[1].start()
    copies[2].start()
    slots_ref[:, :, 0:128] = jnp.full((slots_ref.shape[0], BLK, 128), EMPTY, BF16)
    for b in range(height // BLK):
        where = dest_ref[b]

        @pl.when(where >= 0)
        def _():
            slots_ref[where] = act_ref[b * BLK : (b + 1) * BLK, :].astype(BF16)

    for copy in copies:
        copy.wait()


def find_senders(flags_ref, table_ref):
    for k in range(table_ref.shape[0]):
        table_ref[k] = 0

    def look(s, count):
        sends = flags_ref[s] > 0

        @pl.when(sends)
        def _():
            table_ref[count] = s

        return count + jnp.where(sends, 1, 0)

    lax.fori_loop(0, flags_ref.shape[0], look, jnp.int32(0))


def scatter_kernel(flags_ref, cot_ref, slots_ref, table_ref):
    find_senders(flags_ref, table_ref)
    for k in range(cot_ref.shape[0] // BLK):
        base = k // 4 * 16
        rows = cot_ref[base : base + 16, :].astype(F32)
        low = k % 4 * BLK
        slots_ref[table_ref[k]] = rows[low : low + BLK, :].astype(BF16)


def load_weight(place_ref, pieces, weight_ref, sems):
    count = len(pieces) // 2
    width = pieces[0].shape[1]
    core = place_ref[0]
    groups, row = [], 0
    for i in range(count):
        rows = pieces[i].shape[0]
        copies = []
        for h in range(2):
            start = core * width if h == 0 else (1 - core) * width
            target = weight_ref.at[pl.ds(row, rows), pl.ds(pl.multiple_of(start, 128), width)]
            copies.append(pltpu.make_async_copy(pieces[h * count + i], target, sems.at[2 * i + h]))
            copies[h].start()
        groups.append((row, rows, copies))
        row += rows
    return groups


def block_place(place_ref, owner, blocks):
    ny = blocks // (2 * NX)
    oz, ox, oy = owner // (ny * NX), owner // ny % NX, owner % ny
    return ((ox - place_ref[1] + NX) % NX * 2 + oz) * ny + oy


def backward_kernel(
    dest_ref, place_ref, order_ref,
    kernel_ref, gain_ref, inv_ref, slots_ref,
    frames_hbm, unit_hbm, factor_hbm, shift_hbm, p0, p1, p2, p3, p4, q0, q1, q2, q3, q4,
    frame_ref, term_ref,
    frames_ref, unit_ref, factor_ref, shift_ref,
    home_ref, homeb_ref, weight_ref, raw_ref, sorted_ref, grad_ref, moved_ref, sum_ref, sems,
):
    taps = kernel_ref.shape[0]
    height, columns = frames_ref.shape
    blocks = order_ref.shape[0]
    size = columns // blocks
    groups = load_weight(place_ref, (p0, p1, p2, p3, p4, q0, q1, q2, q3, q4), weight_ref, sems)
    saved = [(unit_hbm, unit_ref), (factor_hbm, factor_ref), (shift_hbm, shift_ref), (frames_hbm, frames_ref)]
    late = [pltpu.make_async_copy(a, b, sems.at[2 * len(groups) + i]) for i, (a, b) in enumerate(saved)]
    for copy in late:
        copy.start()
    for b in range(height // BLK):
        where = dest_ref[b]
        rows = slots_ref[jnp.maximum(where, 0)].astype(F32)
        home_ref[b * BLK : (b + 1) * BLK, :] = jnp.where(where >= 0, rows, 0.0)
    homeb_ref[...] = home_ref[...].astype(BF16)
    for row, rows, copies in groups:
        for copy in copies:
            copy.wait()
        raw_ref[row : row + rows, :] = lax.dot_general(
            weight_ref[row : row + rows, :], homeb_ref[...], (((1,), (1,)), ((), ())), preferred_element_type=F32
        )
    for b in range(blocks):
        at = pl.multiple_of(block_place(place_ref, order_ref[b], blocks) * size, 8)
        sorted_ref[b * size : (b + 1) * size, :] = raw_ref[pl.ds(at, size), :]

    def turn(i, carry):
        at = pl.ds(pl.multiple_of(i * CHUNK, CHUNK), CHUNK)
        home_ref[:, at] = sorted_ref[at, :].astype(BF16).T.astype(F32)
        return carry

    lax.fori_loop(0, columns // CHUNK, turn, 0)
    for copy in late:
        copy.wait()
    step = 16
    gain = gain_ref[...]

    def norm(i, total):
        at = pl.ds(pl.multiple_of(i * step, step), step)
        unit = unit_ref[at, :]
        slope = home_ref[at, :] * factor_ref[at, :]
        along = slope * unit
        total = total + along[0:8] + along[8:16]
        slope = slope * gain
        mean_slope = jnp.mean(slope, axis=1, keepdims=True)
        mean_unit = jnp.mean(along * gain, axis=1, keepdims=True)
        grad_ref[at, :] = (inv_ref[at, 0:1] * (slope - mean_slope - unit * mean_unit)).astype(BF16)
        return total

    total = lax.fori_loop(0, height // step, norm, jnp.zeros((8, columns), F32))
    term_ref[taps] = jnp.sum(total, axis=0, keepdims=True)
    part = 64

    def conv(i, carry):
        at = pl.ds(pl.multiple_of(i * CHUNK, CHUNK), CHUNK)
        moved_ref[...] = jnp.dot(shift_ref[...], grad_ref[:, at], preferred_element_type=F32)
        for p in range(height // part):
            rows = slice(p * part, (p + 1) * part)
            frames = frames_ref[rows, at].astype(F32)
            out = jnp.zeros((part, CHUNK), F32)
            for j in range(taps):
                tap = taps - 1 - j
                moved = moved_ref[j * height + p * part : j * height + (p + 1) * part, :]
                out = out + kernel_ref[pl.ds(tap, 1), at] * moved
                add = jnp.sum((frames * moved).reshape(part // 8, 8, CHUNK), axis=0)
                if p == 0:
                    sum_ref[tap] = add
                elif p < height // part - 1:
                    sum_ref[tap] = sum_ref[tap] + add
                else:
                    term_ref[tap, :, at] = jnp.sum(sum_ref[tap] + add, axis=0, keepdims=True)
            frame_ref[rows, at] = out.astype(BF16)
        return carry

    lax.fori_loop(0, columns // CHUNK, conv, 0)


def project_kernel(
    flags_ref, place_ref, order_ref,
    slots_ref, p0, p1, p2, p3, p4, q0, q1, q2, q3, q4,
    out_ref,
    table_ref, rows_ref, turned_ref, weight_ref, sems,
):
    blocks = order_ref.shape[0]
    size = weight_ref.shape[0] // blocks
    groups = load_weight(place_ref, (p0, p1, p2, p3, p4, q0, q1, q2, q3, q4), weight_ref, sems)
    find_senders(flags_ref, table_ref)
    for k in range(rows_ref.shape[0] // BLK):
        rows_ref[k * BLK : (k + 1) * BLK, :] = slots_ref[table_ref[k]].astype(F32)
    turned = rows_ref[...].T
    for b in range(blocks):
        at = pl.multiple_of(block_place(place_ref, order_ref[b], blocks) * size, 8)
        turned_ref[pl.ds(at, size), :] = turned[b * size : (b + 1) * size, :]
    rows = turned_ref[...].T.astype(BF16)
    for _, _, copies in groups:
        for copy in copies:
            copy.wait()
    out_ref[...] = jnp.dot(rows, weight_ref[...], preferred_element_type=F32).astype(BF16)


VM = pl.BlockSpec(memory_space=pltpu.VMEM)
SM = pl.BlockSpec(memory_space=pltpu.SMEM)
AN = pl.BlockSpec(memory_space=pl.ANY)
HB = pl.BlockSpec(memory_space=pltpu.HBM)


def call(fn, ins, outs, scratch, mib, name, flops, nbytes, out_specs=None):
    return pl.pallas_call(
        fn,
        in_specs=ins,
        out_specs=out_specs or [VM] * len(outs),
        out_shape=outs,
        scratch_shapes=scratch,
        compiler_params=params(mib),
        cost_estimate=pl.CostEstimate(flops=flops, transcendentals=0, bytes_accessed=nbytes),
        name=name,
    )


def exchange(x, axes):
    return lax.all_to_all(x, axes, split_axis=0, concat_axis=0, tiled=True)


def body(frames, lengths, destination, kernel, norm_gain, master, moment, second, gradient, bucket_order, cotangent):
    height, columns = frames.shape
    taps = kernel.shape[0]
    owners = bucket_order.shape[0]
    half = columns // 2
    core, x = lax.axis_index("c"), lax.axis_index("x")
    dest = destination[0]
    lens = lengths[0]
    place = jnp.stack([core, x]).astype(jnp.int32)
    gain = norm_gain[None, :]

    updated = adam_step(master, moment, second, gradient)
    state = [lax.dynamic_slice_in_dim(a, core * half, half, axis=1) for a in (master, moment, second, gradient)]
    bucket = adam_step(*state).astype(BF16)
    near = lax.axis_size(("zl", "y"))
    line = exchange(jnp.broadcast_to(bucket[None], (near, *bucket.shape)), ("zl", "y")).reshape(-1, half)

    slots = jax.ShapeDtypeStruct((owners, BLK, columns), BF16)
    whole = jax.ShapeDtypeStruct((height, columns), F32)
    shifts = jax.ShapeDtypeStruct((taps * height, height), BF16)
    sent, inv, unit, factor, shifts = call(
        forward_kernel,
        [SM, SM, VM, VM, VM],
        [slots, jax.ShapeDtypeStruct((height, 128), F32), whole, whole, shifts],
        [
            pltpu.VMEM(whole.shape, F32),
            pltpu.VMEM(whole.shape, F32),
            pltpu.VMEM(shifts.shape, BF16),
            pltpu.VMEM(whole.shape, F32),
            pltpu.SemaphoreType.DMA((3,)),
        ],
        60,
        "forward",
        8 * taps * height * height * columns,
        16 * height * columns,
        [VM] * 2 + [HB] * 3,
    )(lens, dest, frames, kernel, gain)
    line, sent = lax.optimization_barrier((line, sent))
    act_slots = exchange(sent, DP)

    nx = lax.axis_size("x")
    ahead = [((i + 1) % nx, i) for i in range(nx)]
    behind = [(i, (i + 1) % nx) for i in range(nx)]
    swap = [(0, 1), (1, 0)]
    flags = (act_slots[:, 0, 0] > EMPTY / 2).astype(jnp.int32)
    next_x, last_x = lax.ppermute(line, "x", ahead), lax.ppermute(line, "x", behind)
    line_c = lax.ppermute(line, "c", swap)
    (cot_sent,) = call(
        scatter_kernel, [SM, VM], [slots], [pltpu.SMEM((owners,), jnp.int32)], 60, "scatter", 0, 6 * cotangent.size
    )(flags, cotangent)
    cot_sent, next_x, last_x, line_c = lax.optimization_barrier((cot_sent, next_x, last_x, line_c))
    cot_slots = exchange(cot_sent, DP)
    part = line.shape[0] // 2
    far_low = lax.ppermute(next_x[:part], "x", ahead)
    far_high = lax.ppermute(last_x[part:], "x", behind)
    next_x, far_low = lax.optimization_barrier((next_x, far_low))
    half_pieces = [line, next_x, far_low, far_high, last_x]
    pieces = half_pieces + [line_c] + [lax.ppermute(piece, "c", swap) for piece in half_pieces[1:]]

    frame_grad, term = call(
        backward_kernel,
        [SM] * 3 + [VM] * 4 + [HB] * 4 + [AN] * 10,
        [
            jax.ShapeDtypeStruct((height, columns), BF16),
            jax.ShapeDtypeStruct((taps + 1, 1, columns), F32),
        ],
        [
            pltpu.VMEM((height, columns), BF16),
            pltpu.VMEM((height, columns), F32),
            pltpu.VMEM((height, columns), F32),
            pltpu.VMEM(shifts.shape, BF16),
            pltpu.VMEM((height, columns), F32),
            pltpu.VMEM((height, columns), BF16),
            pltpu.VMEM((columns, columns), BF16),
            pltpu.VMEM((columns, height), F32),
            pltpu.VMEM((columns, height), F32),
            pltpu.VMEM((height, columns), BF16),
            pltpu.VMEM((taps * height, CHUNK), F32),
            pltpu.VMEM((taps, 8, CHUNK), F32),
            pltpu.SemaphoreType.DMA((14,)),
        ],
        60,
        "backward",
        8 * taps * height * height * columns + 2 * height * columns * columns,
        16 * height * columns + 2 * columns * columns,
    )(dest, place, bucket_order, kernel, gain, inv, cot_slots, frames, unit, factor, shifts, *pieces)

    mine = jnp.sum(exchange(term, NEAR), axis=0, keepdims=True)
    far = lax.axis_size(FAR)
    mine = jnp.sum(exchange(jnp.broadcast_to(mine, (far, 1, columns)), FAR), axis=0, keepdims=True)
    (projected,) = call(
        project_kernel,
        [SM] * 3 + [VM] + [AN] * 10,
        [jax.ShapeDtypeStruct(cotangent.shape, BF16)],
        [
            pltpu.SMEM((owners,), jnp.int32),
            pltpu.VMEM(cotangent.shape, F32),
            pltpu.VMEM(cotangent.shape[::-1], F32),
            pltpu.VMEM((columns, columns), BF16),
            pltpu.SemaphoreType.DMA((10,)),
        ],
        60,
        "project",
        2 * cotangent.size * columns,
        4 * cotangent.size + 2 * columns * columns,
    )(flags, place, bucket_order, act_slots, *pieces)
    mine, projected = lax.optimization_barrier((mine, projected))
    divisor = math.sqrt(lax.axis_size(("zh", "c")) * owners * ROWS)
    sums = exchange(jnp.broadcast_to(mine / divisor, (taps + 1, 1, columns)), NEAR)[:, 0, :]
    return projected, frame_grad, sums[:taps], sums[taps], updated


def solution(mesh):
    fine = Mesh(mesh.devices.reshape(4, 2, 2, NX, 8), ("zh", "c", "zl", "x", "y"))
    rep, dp = ("zh", "c"), ("zl", "x", "y")
    every, rows = P(rep + dp, None), P(dp, None)
    return jax.shard_map(
        body,
        mesh=fine,
        in_specs=(every, every, every, P(), P(), rows, rows, rows, rows, P(), every),
        out_specs=(every, every, P(), P(), rows),
        check_vma=False,
    )
```
